32 devices in a mesh: dp: 16 (over z, y, core), mp: 2 (over x).
Axes of the slice: x: 2, y: 2, z: 4, core: 2. Of those that a mesh axis runs over, the one named last changes fastest.
Arguments:
- inputs: bfloat16 [8192, 2048], P('dp', 'mp'), may hold values from -6 to 6
- grad_moved: bfloat16 [8192, 2048], P('dp', 'mp'), may hold values from -6 to 6
- moved: int32 [16, 4], P('dp'), may hold values from 0 to 1, as said below
- segments: int32 [8192], P('dp'), may hold values from 0 to 511, as said below
- input_norm_gain: float32 [2048], replicated, may hold values from 0.5 to 1.5
- proj_in: bfloat16 [2048, 3072], P(None, 'mp'), may hold values from -0.125 to 0.125
- proj_out: bfloat16 [1024, 2048], P('mp'), may hold values from -0.1875 to 0.1875
Outputs:
- input_gradient: bfloat16 [8192, 2048], P('dp', 'mp')
- grad_proj_in: float32 [2048, 3072], P('dp', 'mp')
- grad_proj_out: float32 [1024, 2048], P('mp', 'dp')
The draws below stay inside these ranges and needn't reach their ends.
Inputs may be any that keep to these rules, and one draw needn't show every extreme that they name: moved[g] equals moved[g XOR (8)] for every group g: blocks are swapped between partner groups slot for slot. `segments`: within each group of 512 rows the history numbers start at 0 on its first row, never fall and rise by at most one from row to row; histories never cross groups; in some group every event is a history of its own.
All inputs are finite; a program needn't handle non-finite values.
Results may differ from the reference program's by a relative error of at most 0.011.
Values may be sent and summed in bfloat16 or wider, within the bound.
A program may use at most 128 MiB of HBM per device.

```python
import jax
import jax.numpy as jnp
from jax import lax

D = 2048
HEADS = 8
DV = 128
DQK = 64
BLOCK = 128
ROWS_DEV = 512
TOKENS = 8192
NBLK = 4
HPD = 4
N_DP = 16
N_MP = 2


def draw_moved(key, part):
    half = TOKENS // ROWS_DEV // 2
    flags = jax.random.randint(jax.random.fold_in(key, 11), (half, NBLK), 0, 2).astype(jnp.int32)
    return jnp.concatenate([flags, flags], axis=0)


def draw_segments(key, part):
    groups = TOKENS // ROWS_DEV
    level = jax.random.randint(jax.random.fold_in(key, 21), (groups, 1), 0, 6)
    picks = jax.random.randint(jax.random.fold_in(key, 22), (groups, ROWS_DEV), 0, 1024)
    special = jax.random.randint(jax.random.fold_in(key, 23), (), 0, groups)
    starts = picks < jnp.right_shift(256, level)
    order = jnp.arange(ROWS_DEV, dtype=jnp.int32)[None, :]
    which = jnp.arange(groups, dtype=jnp.int32)[:, None]
    starts = jnp.where(order == 0, True, starts)
    starts = jnp.where(which == special, True, starts).astype(jnp.int32)
    ident = jnp.cumsum(starts, axis=1) - 1
    return ident.reshape(TOKENS).astype(jnp.int32)


def strengthened(drawn, own_key, source, target, shards_of, factor):
    owner, partner = [(jnp.arange(drawn.shape[dim]) // (drawn.shape[dim] // shards_of)).reshape([-1 if axis == dim else 1 for axis in range(drawn.ndim)]) for dim in (source, target)]
    chosen = jax.random.permutation(own_key, shards_of)[partner]
    strong = (owner == chosen) | (owner == (partner + shards_of // 2) % shards_of)
    return jnp.where(strong, factor * drawn, drawn)


def block_scale(own_key, shape, shards, low, top_value):
    factor_of, own = 1.0, jax.random.fold_in(own_key, 6)
    for dim, shards_of in shards:
        steps = jnp.exp(jax.random.uniform(jax.random.fold_in(own, dim), (shards_of,), jnp.float32, low / len(shards), top_value / len(shards)))
        factor_of = factor_of * jnp.repeat(steps, shape[dim] // shards_of).reshape([-1 if axis == dim else 1 for axis in range(len(shape))])
    return factor_of


def noise(stream_key, dims, deviation, bound, pieces=(), held_as=jnp.bfloat16):
    array = deviation * jax.random.normal(stream_key, dims, jnp.float32)
    if pieces:
        array = array * block_scale(stream_key, dims, pieces, -0.22, 0.18)
    return jnp.clip(array, -bound, bound).astype(held_as)


def gaussian_with(stream_key, shape, spread, bound, shards, heavy, kind=jnp.bfloat16):
    values = spread * jax.random.normal(stream_key, shape, jnp.float32)
    if shards:
        values = values * block_scale(stream_key, shape, shards, -0.22, 0.18)
    return jnp.clip(strengthened(values, jax.random.fold_in(stream_key, 3), *heavy), -bound, bound).astype(kind)


def setup_inputs(seed: int = 0) -> dict:
    splits = jax.random.split(jax.random.key(seed), 8)
    return {
        "inputs": gaussian_with(splits[0], (TOKENS, D), 1.0, 6.0, ((0, 16), (1, 2)), (0, 1, 16, 2.0)),
        "grad_moved": gaussian_with(splits[1], (TOKENS, D), 1.0, 6.0, ((0, 16), (1, 2)), (0, 1, 16, 2.0)),
        "moved": draw_moved(jax.random.fold_in(splits[7], 71), 0),
        "segments": draw_segments(jax.random.fold_in(splits[7], 71), 0),
        "input_norm_gain": jnp.clip(1.0 + 0.1 * jax.random.normal(splits[4], (D,), jnp.float32), 0.5, 1.5),
        "proj_in": noise(splits[5], (D, HEADS * (2 * DV + 2 * DQK)), D ** -0.5, 0.125, ((1, 2),)),
        "proj_out": noise(splits[6], (HEADS * DV, D), (HEADS * DV) ** -0.5, 0.1875, ((0, 2),)),
    }


epsilon = 1e-05
head_floor = 1.0

def head_pass(act_dev, seg_dev, mix_dev):
    span = 2 * DV + 2 * DQK
    rows = act_dev.shape[0]
    parts = act_dev.reshape(rows, HEADS, span).astype(jnp.float32)
    u_vals = parts[:, :, :DV]
    v_vals = parts[:, :, DV:2 * DV]
    q_vals = parts[:, :, 2 * DV:2 * DV + DQK]
    k_vals = parts[:, :, 2 * DV + DQK:]
    order = jnp.arange(rows, dtype=jnp.int32)
    visible = ((seg_dev[:, None] == seg_dev[None, :]) & (order[None, :] <= order[:, None])).astype(jnp.float32)
    scores = jnp.einsum('qhd,khd->hqk', q_vals, k_vals)
    sig_s = jax.nn.sigmoid(scores)
    attend = (scores * sig_s * visible).astype(jnp.bfloat16).astype(jnp.float32)
    slope = sig_s * (1.0 + scores * (1.0 - sig_s))
    outvals = jnp.einsum('hqk,khd->qhd', attend, v_vals)
    mean_shifted = outvals - lax.optimization_barrier(jnp.mean(outvals, axis=-1, keepdims=True))
    head_inv = lax.rsqrt(lax.optimization_barrier(jnp.mean(mean_shifted * mean_shifted, axis=-1, keepdims=True)) + head_floor)
    onorm = mean_shifted * head_inv
    mixed = (onorm * u_vals).astype(jnp.bfloat16)
    grad_mix = mix_dev.reshape(rows, HEADS, DV)
    grad_u = grad_mix * onorm
    gon = grad_mix * u_vals
    grad_o = (head_inv * (gon - lax.optimization_barrier(jnp.mean(gon, axis=-1, keepdims=True)) - onorm * lax.optimization_barrier(jnp.mean(gon * onorm, axis=-1, keepdims=True)))).astype(jnp.bfloat16).astype(jnp.float32)
    grad_att = jnp.einsum('qhd,khd->hqk', grad_o, v_vals)
    grad_v = jnp.einsum('hqk,qhd->khd', attend, grad_o)
    grad_scores = (grad_att * visible * slope).astype(jnp.bfloat16).astype(jnp.float32)
    grad_q = jnp.einsum('hqk,khd->qhd', grad_scores, k_vals)
    grad_k = jnp.einsum('hqk,qhd->khd', grad_scores, q_vals)
    grad_act = jnp.concatenate([grad_u, grad_v, grad_q, grad_k], axis=-1).reshape(rows, HEADS * span)
    return (mixed.reshape(rows, HEADS * DV), grad_act)

def reference(inputs, grad_moved, moved, segments, input_norm_gain, proj_in, proj_out):
    groups = N_DP
    span = 2 * DV + 2 * DQK
    blocks = grad_moved.reshape(groups, NBLK, BLOCK, D)
    partner = jnp.concatenate([blocks[groups // 2:], blocks[:groups // 2]], axis=0)
    output_gradient = jnp.where(moved[:, :, None, None] == 1, partner, blocks).reshape(TOKENS, D)
    xfull = inputs.astype(jnp.float32)
    mean_shifted = xfull - lax.optimization_barrier(jnp.mean(xfull, axis=1, keepdims=True))
    inverse_deviation = lax.rsqrt(lax.optimization_barrier(jnp.mean(mean_shifted * mean_shifted, axis=1, keepdims=True)) + epsilon)
    standardized_input = mean_shifted * inverse_deviation
    normalized_rows = (standardized_input * input_norm_gain[None, :]).astype(jnp.bfloat16)
    pre = jnp.dot(normalized_rows, proj_in, preferred_element_type=jnp.float32)
    sig_p = jax.nn.sigmoid(pre)
    act = (pre * sig_p).astype(jnp.bfloat16)
    grad_mix = lax.dot_general(output_gradient, proj_out, (((1,), (1,)), ((), ())), preferred_element_type=jnp.float32)
    mixed, grad_act = lax.map(lambda item: head_pass(item[0], item[1], item[2]), (act.reshape(groups, ROWS_DEV, HEADS * span), segments.reshape(groups, ROWS_DEV), grad_mix.reshape(groups, ROWS_DEV, HEADS * DV)))
    mixed = mixed.reshape(TOKENS, HEADS * DV)
    grad_act = grad_act.reshape(TOKENS, HEADS * span)
    grad_pre = (grad_act * sig_p * (1.0 + pre * (1.0 - sig_p))).astype(jnp.bfloat16)
    grad_proj_out = lax.dot_general(mixed, output_gradient, (((0,), (0,)), ((), ())), preferred_element_type=jnp.float32)
    grad_proj_in = lax.dot_general(normalized_rows, grad_pre, (((0,), (0,)), ((), ())), preferred_element_type=jnp.float32)
    width = HPD * span
    grad_normed = jnp.zeros((TOKENS, D), jnp.float32)
    for group in range(N_MP):
        term = lax.dot_general(grad_pre[:, group * width:(group + 1) * width], proj_in[:, group * width:(group + 1) * width], (((1,), (1,)), ((), ())), preferred_element_type=jnp.float32)
        rounded = lax.optimization_barrier(term.astype(jnp.bfloat16))
        grad_normed = grad_normed + rounded.astype(jnp.float32)
    gain_scaled = grad_normed * input_norm_gain[None, :]
    input_gradient = output_gradient.astype(jnp.float32) + inverse_deviation * (gain_scaled - lax.optimization_barrier(jnp.mean(gain_scaled, axis=1, keepdims=True)) - standardized_input * lax.optimization_barrier(jnp.mean(gain_scaled * standardized_input, axis=1, keepdims=True)))
    return (input_gradient.astype(jnp.bfloat16), grad_proj_in, grad_proj_out)
```

```python
import jax
import jax.numpy as jnp
from jax import lax
from jax.experimental import pallas as pl
from jax.experimental.pallas import tpu as pltpu
from jax.sharding import PartitionSpec as P

DV = 128
DQK = 64
BLOCK = 128


epsilon = 1e-05
head_floor = 1.0


def swapped(block, axis, apart):
    count = lax.axis_size(axis)
    route = []
    for low in range(count):
        high = low | 1 << apart
        if high != low and high < count:
            route += [(low, high), (high, low)]
    return lax.ppermute(block, axis, route)


def gathered(block):
    if lax.axis_size("mp") != 2:
        return lax.all_gather(block, "mp", axis=1, tiled=True)
    other = lax.ppermute(block, "mp", [(0, 1), (1, 0)])
    first = lax.axis_index("mp") == 0
    return jnp.concatenate(
        [jnp.where(first, block, other), jnp.where(first, other, block)], axis=1
    )


def forward_heads(acts, visible, heads_here):
    span = 2 * DV + 2 * DQK
    rows = acts.shape[0]
    parts = acts.reshape(rows, heads_here, span)
    u_vals = parts[:, :, :DV]
    v_vals = parts[:, :, DV : 2 * DV]
    q_vals = parts[:, :, 2 * DV : 2 * DV + DQK]
    k_vals = parts[:, :, 2 * DV + DQK :]
    scores = jnp.einsum("qhd,khd->hqk", q_vals, k_vals, preferred_element_type=jnp.float32)
    sig_s = jax.nn.sigmoid(scores)
    attend = (scores * sig_s * visible[None]).astype(jnp.bfloat16)
    slope = sig_s * (1.0 + scores * (1.0 - sig_s))
    outvals = jnp.einsum("hqk,khd->qhd", attend, v_vals, preferred_element_type=jnp.float32)
    mean_shifted = outvals - jnp.mean(outvals, axis=-1, keepdims=True)
    head_inv = lax.rsqrt(jnp.mean(mean_shifted * mean_shifted, axis=-1, keepdims=True) + head_floor)
    onorm = mean_shifted * head_inv
    mixed = (onorm * u_vals).astype(jnp.bfloat16).reshape(rows, heads_here * DV)
    saved = (u_vals, v_vals, q_vals, k_vals, attend, slope, onorm, head_inv)
    return (mixed, saved)


def backward_heads(saved, grad_mix, visible, heads_here):
    u_vals, v_vals, q_vals, k_vals, attend, slope, onorm, head_inv = saved
    rows = grad_mix.shape[0]
    grad_mixr = grad_mix.reshape(rows, heads_here, DV)
    grad_u = grad_mixr * onorm
    gon = grad_mixr * u_vals
    grad_o = (
        head_inv
        * (
            gon
            - jnp.mean(gon, axis=-1, keepdims=True)
            - onorm * jnp.mean(gon * onorm, axis=-1, keepdims=True)
        )
    ).astype(jnp.bfloat16)
    grad_att = jnp.einsum("qhd,khd->hqk", grad_o, v_vals, preferred_element_type=jnp.float32)
    grad_v = jnp.einsum("hqk,qhd->khd", attend, grad_o, preferred_element_type=jnp.float32)
    grad_scores = (grad_att * visible[None] * slope).astype(jnp.bfloat16)
    grad_q = jnp.einsum("hqk,khd->qhd", grad_scores, k_vals, preferred_element_type=jnp.float32)
    grad_k = jnp.einsum("hqk,qhd->khd", grad_scores, q_vals, preferred_element_type=jnp.float32)
    grad_act = jnp.concatenate([grad_u, grad_v, grad_q, grad_k], axis=-1)
    return grad_act.reshape(rows, heads_here * (2 * DV + 2 * DQK))


MESH = pl.DeviceIdType.MESH


def reduce_kernel(
    normed_ref, pre_ref, dy_ref, mixed_ref, term_ref, sums_ref,
    gin_ref, gout_ref, rterm_ref, rsums_ref,
    own, send_c, recv_c, send_y, recv_y, keep_y, send_z, from_low, from_high, land_t, land_s,
    sem_cs, sem_cr, sem_ys, sem_yr, sem_zs, sem_low, sem_high, sem_xs, sem_xr,
):
    wide = pre_ref.shape[1]
    d = lax.axis_index("dp")
    x = lax.axis_index("mp")
    z = d // 4
    y = (d // 2) % 2
    c = d % 2
    upper = z // 2
    inner = (z + upper) % 2
    core_peer = d + 1 - 2 * c
    y_peer = d + 2 - 4 * y

    barrier = pltpu.get_barrier_semaphore()

    def greet(where):
        pl.semaphore_signal(barrier, inc=1, device_id=where, device_id_type=MESH)

    greet({"dp": core_peer})
    greet({"dp": y_peer})
    greet({"mp": 1 - x})

    @pl.when(z > 0)
    def _():
        greet({"dp": d - 4})

    @pl.when(z < 3)
    def _():
        greet({"dp": d + 4})

    pl.semaphore_wait(barrier, 3 + (z + 3) // 4 + (6 - z) // 4)

    def remote(src, dst, send_sem, recv_sem, where):
        return pltpu.make_async_remote_copy(
            src_ref=src, dst_ref=dst, send_sem=send_sem, recv_sem=recv_sem,
            device_id=where, device_id_type=MESH,
        )

    cross_t = remote(term_ref, land_t, sem_xs.at[0], sem_xr.at[0], {"mp": 1 - x})
    cross_s = remote(sums_ref, land_s, sem_xs.at[1], sem_xr.at[1], {"mp": 1 - x})
    cross_t.start()
    cross_s.start()

    def target(k):
        v = (3 - k) + (k // 2) * inner * (2 * k - 5)
        return (1 - upper) * v + upper * (3 - v)

    def product(slot, core):
        k = slot % 4
        side = (1 - slot // 4) * (1 - y) + (slot // 4) * y
        chunk = target(k) * 4 + side * 2 + core
        cols = pl.ds(pl.multiple_of(chunk * 128, 128), 128)
        left = lax.dot_general(
            normed_ref[:, cols], pre_ref[...], (((0,), (0,)), ((), ())),
            preferred_element_type=jnp.float32,
        )
        right = lax.dot_general(
            dy_ref[:, cols], mixed_ref[...], (((0,), (0,)), ((), ())),
            preferred_element_type=jnp.float32,
        )
        return left, right

    def to_core(slot):
        return remote(
            send_c.at[slot], recv_c.at[slot], sem_cs.at[slot], sem_cr.at[slot], {"dp": core_peer}
        )

    def to_y(k):
        return remote(send_y.at[k], recv_y.at[k], sem_ys.at[k], sem_yr.at[k], {"dp": y_peer})

    def issue(slot):
        left, right = product(slot, 1 - c)
        send_c[slot, :, :wide] = left.astype(jnp.bfloat16)
        send_c[slot, :, wide:] = right.astype(jnp.bfloat16)
        to_core(slot).start()

    issue(0)

    def step(slot, carry):
        @pl.when(slot < 7)
        def _():
            issue(slot + 1)

        left, right = product(slot, c)
        own[:, :wide] = left
        own[:, wide:] = right
        to_core(slot).wait_recv()

        @pl.when(slot < 4)
        def _():
            send_y[slot] = (own[...] + recv_c[slot].astype(jnp.float32)).astype(jnp.bfloat16)
            to_y(slot).start()

        @pl.when(slot >= 4)
        def _():
            keep_y[slot - 4] = (own[...] + recv_c[slot].astype(jnp.float32)).astype(jnp.bfloat16)

        return carry

    lax.fori_loop(0, 8, step, 0)

    def up(k, t):
        return remote(send_z.at[k], from_low.at[t], sem_zs.at[k], sem_low.at[t], {"dp": d + 4})

    def down(k, t):
        return remote(send_z.at[k], from_high.at[t], sem_zs.at[k], sem_high.at[t], {"dp": d - 4})

    def along(k, carry):
        t = target(k)
        to_y(k).wait_recv()

        @pl.when(t == z)
        def _():
            own[...] = keep_y[k].astype(jnp.float32) + recv_y[k].astype(jnp.float32)

        def forward(arrived, sem, present, copy):
            @pl.when(present)
            def _():
                pltpu.make_async_copy(arrived.at[t], arrived.at[t], sem.at[t]).wait()
                send_z[k] = (
                    keep_y[k].astype(jnp.float32)
                    + recv_y[k].astype(jnp.float32)
                    + arrived[t].astype(jnp.float32)
                ).astype(jnp.bfloat16)

            @pl.when(jnp.logical_not(present))
            def _():
                send_z[k] = (
                    keep_y[k].astype(jnp.float32) + recv_y[k].astype(jnp.float32)
                ).astype(jnp.bfloat16)

            copy.start()

        @pl.when(t > z)
        def _():
            forward(from_low, sem_low, z > 0, up(k, t))

        @pl.when(t < z)
        def _():
            forward(from_high, sem_high, z < 3, down(k, t))

        return carry

    lax.fori_loop(0, 4, along, 0)

    @pl.when(z > 0)
    def _():
        pltpu.make_async_copy(from_low.at[z], from_low.at[z], sem_low.at[z]).wait()
        own[...] += from_low[z].astype(jnp.float32)

    @pl.when(z < 3)
    def _():
        pltpu.make_async_copy(from_high.at[z], from_high.at[z], sem_high.at[z]).wait()
        own[...] += from_high[z].astype(jnp.float32)

    gin_ref[...] = own[:, :wide]
    gout_ref[...] = own[:, wide:]
    cross_t.wait()
    cross_s.wait()
    rterm_ref[...] = land_t[...]
    rsums_ref[...] = land_s[...]

    def drain(slot, carry):
        to_core(slot).wait_send()
        return carry

    lax.fori_loop(0, 8, drain, 0)

    def drain_far(k, carry):
        to_y(k).wait_send()
        t = target(k)

        @pl.when(t > z)
        def _():
            up(k, t).wait_send()

        @pl.when(t < z)
        def _():
            down(k, t).wait_send()

        return carry

    lax.fori_loop(0, 4, drain_far, 0)


def reduced(normed, grad_pre, full_dy, mixed, term, sums):
    wide, narrow = grad_pre.shape[1], mixed.shape[1]
    total = wide + narrow
    low, full = jnp.bfloat16, jnp.float32
    return pl.pallas_call(
        reduce_kernel,
        out_shape=(
            jax.ShapeDtypeStruct((128, wide), full),
            jax.ShapeDtypeStruct((128, narrow), full),
            jax.ShapeDtypeStruct(term.shape, low),
            jax.ShapeDtypeStruct(sums.shape, full),
        ),
        in_specs=[pl.BlockSpec(memory_space=pltpu.VMEM)] * 6,
        out_specs=[pl.BlockSpec(memory_space=pltpu.VMEM)] * 4,
        scratch_shapes=[
            pltpu.VMEM((128, total), full),
            pltpu.VMEM((8, 128, total), low),
            pltpu.VMEM((8, 128, total), low),
            pltpu.VMEM((4, 128, total), low),
            pltpu.VMEM((4, 128, total), low),
            pltpu.VMEM((4, 128, total), low),
            pltpu.VMEM((4, 128, total), low),
            pltpu.VMEM((4, 128, total), low),
            pltpu.VMEM((4, 128, total), low),
            pltpu.VMEM(term.shape, low),
            pltpu.VMEM(sums.shape, full),
            pltpu.SemaphoreType.DMA((8,)),
            pltpu.SemaphoreType.DMA((8,)),
            pltpu.SemaphoreType.DMA((4,)),
            pltpu.SemaphoreType.DMA((4,)),
            pltpu.SemaphoreType.DMA((4,)),
            pltpu.SemaphoreType.DMA((4,)),
            pltpu.SemaphoreType.DMA((4,)),
            pltpu.SemaphoreType.DMA((2,)),
            pltpu.SemaphoreType.DMA((2,)),
        ],
        compiler_params=pltpu.CompilerParams(
            collective_id=0, has_side_effects=True, vmem_limit_bytes=60 * 1024 * 1024
        ),
    )(normed, grad_pre, full_dy, mixed, term, sums)


def on_device(inputs, grad_moved, moved, segments, input_norm_gain, proj_in, proj_out):
    rows = inputs.shape[0]
    span = 2 * DV + 2 * DQK
    heads_here = proj_in.shape[1] // span
    top_bit = lax.axis_size("dp").bit_length() - 2
    blocks = rows // BLOCK
    mine = [grad_moved[j * BLOCK : (j + 1) * BLOCK] for j in range(blocks)]
    theirs = [swapped(block, "dp", top_bit) for block in mine]
    full_x = gathered(inputs)
    after, returned = full_x, []
    for j in range(blocks):
        landed, after = lax.optimization_barrier((theirs[j], after))
        full_x = after if j == 0 else full_x
        after = jnp.where(moved[0, j] == 1, landed, mine[j])
        returned.append(gathered(after))
    full_dy = jnp.concatenate(returned, axis=0)
    xfull = full_x.astype(jnp.float32)
    mean_shifted = xfull - jnp.mean(xfull, axis=1, keepdims=True)
    inverse_deviation = lax.rsqrt(
        jnp.mean(mean_shifted * mean_shifted, axis=1, keepdims=True) + epsilon
    )
    standardized_input = mean_shifted * inverse_deviation
    normalized_rows = (standardized_input * input_norm_gain[None, :]).astype(jnp.bfloat16)
    pre = jnp.dot(normalized_rows, proj_in, preferred_element_type=jnp.float32)
    sig_p = jax.nn.sigmoid(pre)
    acts = (pre * sig_p).astype(jnp.bfloat16)
    grad_mix = lax.dot_general(
        full_dy, proj_out, (((1,), (1,)), ((), ())), preferred_element_type=jnp.float32
    )
    order = jnp.arange(rows, dtype=jnp.int32)
    visible = (
        (segments[:, None] == segments[None, :]) & (order[None, :] <= order[:, None])
    ).astype(jnp.float32)
    mixed, saved = forward_heads(acts, visible, heads_here)
    grad_act = backward_heads(saved, grad_mix, visible, heads_here)
    grad_pre = (grad_act * sig_p * (1.0 + pre * (1.0 - sig_p))).astype(jnp.bfloat16)
    local = inputs.shape[1]
    offset = lax.axis_index("mp") * local
    normed_term = lax.dot_general(
        grad_pre, proj_in, (((1,), (1,)), ((), ())), preferred_element_type=jnp.float32
    ).astype(jnp.bfloat16)
    term_scaled = normed_term.astype(jnp.float32) * input_norm_gain[None, :]
    sums = jnp.stack([jnp.sum(term_scaled, axis=1), jnp.sum(term_scaled * standardized_input, axis=1)])
    if lax.axis_size("mp") == 2 and lax.axis_size("dp") == 16:
        sent = lax.dynamic_slice_in_dim(normed_term, local - offset, local, 1)
        kept = lax.dynamic_slice_in_dim(normed_term, offset, local, 1)
        grad_proj_in, grad_proj_out, other_term, other_sums = reduced(
            normalized_rows, grad_pre, full_dy, mixed, sent, sums
        )
        grad_proj_out = grad_proj_out.T
        sums = sums + other_sums
        grad_normed = kept.astype(jnp.float32) + other_term.astype(jnp.float32)
    else:
        partial_out = lax.dot_general(
            mixed, full_dy, (((0,), (0,)), ((), ())), preferred_element_type=jnp.float32
        )
        grad_proj_out = lax.psum_scatter(
            partial_out.astype(jnp.bfloat16), "dp", scatter_dimension=1, tiled=True
        ).astype(jnp.float32)
        partial_in = lax.dot_general(
            normalized_rows, grad_pre, (((0,), (0,)), ((), ())), preferred_element_type=jnp.float32
        )
        grad_proj_in = lax.psum_scatter(
            partial_in.astype(jnp.bfloat16), "dp", scatter_dimension=0, tiled=True
        ).astype(jnp.float32)
        sums = lax.psum(sums, "mp")
        grad_normed = lax.psum_scatter(
            normed_term, "mp", scatter_dimension=1, tiled=True
        ).astype(jnp.float32)
    means = sums / standardized_input.shape[1]
    here = lambda array: lax.dynamic_slice_in_dim(array, offset, local, 1)
    grad_here = here(full_dy).astype(jnp.float32) + inverse_deviation * (
        grad_normed * here(input_norm_gain[None, :])
        - means[0][:, None]
        - here(standardized_input) * means[1][:, None]
    )
    input_gradient = grad_here.astype(jnp.bfloat16)
    return (input_gradient, grad_proj_in, grad_proj_out)


def solution(mesh):
    return jax.shard_map(
        on_device,
        mesh=mesh,
        in_specs=(
            P("dp", "mp"),
            P("dp", "mp"),
            P("dp", None),
            P("dp"),
            P(),
            P(None, "mp"),
            P("mp", None),
        ),
        out_specs=(P("dp", "mp"), P("dp", "mp"), P("mp", "dp")),
        check_vma=False,
    )
```

```python
import jax
import jax.numpy as jnp
from jax import lax
from jax.experimental import pallas as pl
from jax.experimental.pallas import tpu as pltpu
from jax.sharding import PartitionSpec as P

DV = 128
DQK = 64
BLOCK = 128


epsilon = 1e-05
head_floor = 1.0


def swapped(block, axis, apart):
    count = lax.axis_size(axis)
    route = []
    for low in range(count):
        high = low | 1 << apart
        if high != low and high < count:
            route += [(low, high), (high, low)]
    return lax.ppermute(block, axis, route)


def gathered(block):
    return lax.all_gather(block, "mp", axis=1, tiled=True)


def forward_heads(acts, visible, heads_here):
    span = 2 * DV + 2 * DQK
    rows = acts.shape[0]
    parts = acts.reshape(rows, heads_here, span)
    u_vals = parts[:, :, :DV]
    v_vals = parts[:, :, DV : 2 * DV]
    q_vals = parts[:, :, 2 * DV : 2 * DV + DQK]
    k_vals = parts[:, :, 2 * DV + DQK :]
    scores = jnp.einsum("qhd,khd->hqk", q_vals, k_vals, preferred_element_type=jnp.float32)
    sig_s = jax.nn.sigmoid(scores)
    attend = (scores * sig_s * visible[None]).astype(jnp.bfloat16)
    slope = sig_s * (1.0 + scores * (1.0 - sig_s))
    outvals = jnp.einsum("hqk,khd->qhd", attend, v_vals, preferred_element_type=jnp.float32)
    mean_shifted = outvals - jnp.mean(outvals, axis=-1, keepdims=True)
    head_inv = lax.rsqrt(jnp.mean(mean_shifted * mean_shifted, axis=-1, keepdims=True) + head_floor)
    onorm = mean_shifted * head_inv
    mixed = (onorm * u_vals).astype(jnp.bfloat16).reshape(rows, heads_here * DV)
    saved = (u_vals, v_vals, q_vals, k_vals, attend, slope, onorm, head_inv)
    return (mixed, saved)


def backward_heads(saved, grad_mix, visible, heads_here):
    u_vals, v_vals, q_vals, k_vals, attend, slope, onorm, head_inv = saved
    rows = grad_mix.shape[0]
    grad_mixr = grad_mix.reshape(rows, heads_here, DV)
    grad_u = grad_mixr * onorm
    gon = grad_mixr * u_vals
    grad_o = (
        head_inv
        * (
            gon
            - jnp.mean(gon, axis=-1, keepdims=True)
            - onorm * jnp.mean(gon * onorm, axis=-1, keepdims=True)
        )
    ).astype(jnp.bfloat16)
    grad_att = jnp.einsum("qhd,khd->hqk", grad_o, v_vals, preferred_element_type=jnp.float32)
    grad_v = jnp.einsum("hqk,qhd->khd", attend, grad_o, preferred_element_type=jnp.float32)
    grad_scores = (grad_att * visible[None] * slope).astype(jnp.bfloat16)
    grad_q = jnp.einsum("hqk,khd->qhd", grad_scores, k_vals, preferred_element_type=jnp.float32)
    grad_k = jnp.einsum("hqk,qhd->khd", grad_scores, q_vals, preferred_element_type=jnp.float32)
    grad_act = jnp.concatenate([grad_u, grad_v, grad_q, grad_k], axis=-1)
    return grad_act.reshape(rows, heads_here * (2 * DV + 2 * DQK))


MESH = pl.DeviceIdType.MESH


def reduce_kernel(
    normed_ref, pre_ref, dy_ref, mixed_ref, term_ref, sums_ref,
    gin_ref, gout_ref, rterm_ref, rsums_ref,
    own, send_c, recv_c, send_y, recv_y, keep_y, send_z, from_low, from_high, land_t, land_s,
    sem_cs, sem_cr, sem_ys, sem_yr, sem_zs, sem_low, sem_high, sem_xs, sem_xr,
):
    wide = pre_ref.shape[1]
    d = lax.axis_index("dp")
    x = lax.axis_index("mp")
    z = d // 4
    y = (d // 2) % 2
    c = d % 2
    upper = z // 2
    inner = (z + upper) % 2
    core_peer = d + 1 - 2 * c
    y_peer = d + 2 - 4 * y

    barrier = pltpu.get_barrier_semaphore()

    def greet(where):
        pl.semaphore_signal(barrier, inc=1, device_id=where, device_id_type=MESH)

    greet({"dp": core_peer})
    greet({"dp": y_peer})
    greet({"mp": 1 - x})

    @pl.when(z > 0)
    def _():
        greet({"dp": d - 4})

    @pl.when(z < 3)
    def _():
        greet({"dp": d + 4})

    pl.semaphore_wait(barrier, 3 + (z + 3) // 4 + (6 - z) // 4)

    def remote(src, dst, send_sem, recv_sem, where):
        return pltpu.make_async_remote_copy(
            src_ref=src, dst_ref=dst, send_sem=send_sem, recv_sem=recv_sem,
            device_id=where, device_id_type=MESH,
        )

    cross_t = remote(term_ref, land_t, sem_xs.at[0], sem_xr.at[0], {"mp": 1 - x})
    cross_s = remote(sums_ref, land_s, sem_xs.at[1], sem_xr.at[1], {"mp": 1 - x})
    cross_t.start()
    cross_s.start()

    def target(k):
        v = (3 - k) + (k // 2) * inner * (2 * k - 5)
        return (1 - upper) * v + upper * (3 - v)

    def product(slot, core):
        k = slot % 4
        side = (1 - slot // 4) * (1 - y) + (slot // 4) * y
        chunk = target(k) * 4 + side * 2 + core
        cols = pl.ds(pl.multiple_of(chunk * 128, 128), 128)
        left = lax.dot_general(
            normed_ref[:, cols], pre_ref[...], (((0,), (0,)), ((), ())),
            preferred_element_type=jnp.float32,
        )
        right = lax.dot_general(
            dy_ref[:, cols], mixed_ref[...], (((0,), (0,)), ((), ())),
            preferred_element_type=jnp.float32,
        )
        return left, right

    def to_core(slot):
        return remote(
            send_c.at[slot], recv_c.at[slot], sem_cs.at[slot], sem_cr.at[slot], {"dp": core_peer}
        )

    def to_y(k):
        return remote(send_y.at[k], recv_y.at[k], sem_ys.at[k], sem_yr.at[k], {"dp": y_peer})

    def issue(slot):
        left, right = product(slot, 1 - c)
        send_c[slot, :, :wide] = left.astype(jnp.bfloat16)
        send_c[slot, :, wide:] = right.astype(jnp.bfloat16)
        to_core(slot).start()

    issue(0)

    def step(slot, carry):
        @pl.when(slot < 7)
        def _():
            issue(slot + 1)

        left, right = product(slot, c)
        own[:, :wide] = left
        own[:, wide:] = right
        to_core(slot).wait_recv()

        @pl.when(slot < 4)
        def _():
            send_y[slot] = (own[...] + recv_c[slot].astype(jnp.float32)).astype(jnp.bfloat16)
            to_y(slot).start()

        @pl.when(slot >= 4)
        def _():
            keep_y[slot - 4] = (own[...] + recv_c[slot].astype(jnp.float32)).astype(jnp.bfloat16)

        return carry

    lax.fori_loop(0, 8, step, 0)

    def up(k, t):
        return remote(send_z.at[k], from_low.at[t], sem_zs.at[k], sem_low.at[t], {"dp": d + 4})

    def down(k, t):
        return remote(send_z.at[k], from_high.at[t], sem_zs.at[k], sem_high.at[t], {"dp": d - 4})

    def along(k, carry):
        t = target(k)
        to_y(k).wait_recv()

        @pl.when(t == z)
        def _():
            own[...] = keep_y[k].astype(jnp.float32) + recv_y[k].astype(jnp.float32)

        def forward(arrived, sem, present, copy):
            @pl.when(present)
            def _():
                pltpu.make_async_copy(arrived.at[t], arrived.at[t], sem.at[t]).wait()
                send_z[k] = (
                    keep_y[k].astype(jnp.float32)
                    + recv_y[k].astype(jnp.float32)
                    + arrived[t].astype(jnp.float32)
                ).astype(jnp.bfloat16)

            @pl.when(jnp.logical_not(present))
            def _():
                send_z[k] = (
                    keep_y[k].astype(jnp.float32) + recv_y[k].astype(jnp.float32)
                ).astype(jnp.bfloat16)

            copy.start()

        @pl.when(t > z)
        def _():
            forward(from_low, sem_low, z > 0, up(k, t))

        @pl.when(t < z)
        def _():
            forward(from_high, sem_high, z < 3, down(k, t))

        return carry

    lax.fori_loop(0, 4, along, 0)

    @pl.when(z > 0)
    def _():
        pltpu.make_async_copy(from_low.at[z], from_low.at[z], sem_low.at[z]).wait()
        own[...] += from_low[z].astype(jnp.float32)

    @pl.when(z < 3)
    def _():
        pltpu.make_async_copy(from_high.at[z], from_high.at[z], sem_high.at[z]).wait()
        own[...] += from_high[z].astype(jnp.float32)

    gin_ref[...] = own[:, :wide]
    gout_ref[...] = own[:, wide:]
    cross_t.wait()
    cross_s.wait()
    rterm_ref[...] = land_t[...]
    rsums_ref[...] = land_s[...]

    def drain(slot, carry):
        to_core(slot).wait_send()
        return carry

    lax.fori_loop(0, 8, drain, 0)

    def drain_far(k, carry):
        to_y(k).wait_send()
        t = target(k)

        @pl.when(t > z)
        def _():
            up(k, t).wait_send()

        @pl.when(t < z)
        def _():
            down(k, t).wait_send()

        return carry

    lax.fori_loop(0, 4, drain_far, 0)


def reduced(normed, grad_pre, full_dy, mixed, term, sums):
    wide, narrow = grad_pre.shape[1], mixed.shape[1]
    total = wide + narrow
    low, full = jnp.bfloat16, jnp.float32
    return pl.pallas_call(
        reduce_kernel,
        out_shape=(
            jax.ShapeDtypeStruct((128, wide), full),
            jax.ShapeDtypeStruct((128, narrow), full),
            jax.ShapeDtypeStruct(term.shape, low),
            jax.ShapeDtypeStruct(sums.shape, full),
        ),
        in_specs=[pl.BlockSpec(memory_space=pltpu.VMEM)] * 6,
        out_specs=[pl.BlockSpec(memory_space=pltpu.VMEM)] * 4,
        scratch_shapes=[
            pltpu.VMEM((128, total), full),
            pltpu.VMEM((8, 128, total), low),
            pltpu.VMEM((8, 128, total), low),
            pltpu.VMEM((4, 128, total), low),
            pltpu.VMEM((4, 128, total), low),
            pltpu.VMEM((4, 128, total), low),
            pltpu.VMEM((4, 128, total), low),
            pltpu.VMEM((4, 128, total), low),
            pltpu.VMEM((4, 128, total), low),
            pltpu.VMEM(term.shape, low),
            pltpu.VMEM(sums.shape, full),
            pltpu.SemaphoreType.DMA((8,)),
            pltpu.SemaphoreType.DMA((8,)),
            pltpu.SemaphoreType.DMA((4,)),
            pltpu.SemaphoreType.DMA((4,)),
            pltpu.SemaphoreType.DMA((4,)),
            pltpu.SemaphoreType.DMA((4,)),
            pltpu.SemaphoreType.DMA((4,)),
            pltpu.SemaphoreType.DMA((2,)),
            pltpu.SemaphoreType.DMA((2,)),
        ],
        compiler_params=pltpu.CompilerParams(
            collective_id=0, has_side_effects=True, vmem_limit_bytes=60 * 1024 * 1024
        ),
    )(normed, grad_pre, full_dy, mixed, term, sums)


def gather_kernel(
    x_ref, moved_ref, flags_ref, gain_ref, w_ref,
    fullx_ref, fully_ref, normed_ref, pre_ref, mean_ref, inv_ref,
    land_z, land_x, land_y, chosen,
    sem_zs, sem_zr, sem_xs, sem_xr, sem_ys, sem_yr,
):
    d = lax.axis_index("dp")
    m = lax.axis_index("mp")
    half = x_ref.shape[1]
    partner = (d + 8) % 16
    barrier = pltpu.get_barrier_semaphore()
    pl.semaphore_signal(barrier, inc=1, device_id={"dp": partner}, device_id_type=MESH)
    pl.semaphore_signal(barrier, inc=1, device_id={"mp": 1 - m}, device_id_type=MESH)
    pl.semaphore_wait(barrier, 2)
    here = pl.ds(pl.multiple_of(m * half, half), half)
    there = pl.ds(pl.multiple_of((1 - m) * half, half), half)

    def rows_of(j):
        return pl.ds(pl.multiple_of(j * BLOCK, BLOCK), BLOCK)

    def swap_rows(j):
        return pltpu.make_async_remote_copy(
            src_ref=moved_ref.at[rows_of(j)], dst_ref=land_z.at[j],
            send_sem=sem_zs.at[j], recv_sem=sem_zr.at[j],
            device_id={"dp": partner}, device_id_type=MESH,
        )

    def share_x(j):
        return pltpu.make_async_remote_copy(
            src_ref=x_ref.at[rows_of(j)], dst_ref=land_x.at[j],
            send_sem=sem_xs.at[j], recv_sem=sem_xr.at[j],
            device_id={"mp": 1 - m}, device_id_type=MESH,
        )

    def share_y(j):
        return pltpu.make_async_remote_copy(
            src_ref=chosen.at[j], dst_ref=land_y.at[j],
            send_sem=sem_ys.at[j], recv_sem=sem_yr.at[j],
            device_id={"mp": 1 - m}, device_id_type=MESH,
        )

    def begin(j, carry):
        swap_rows(j).start()
        share_x(j).start()
        return carry

    def block(j, carry):
        rows = rows_of(j)
        share_x(j).wait_recv()
        fullx_ref[rows, here] = x_ref[rows, :]
        fullx_ref[rows, there] = land_x[j]
        wide = fullx_ref[rows, :].astype(jnp.float32)
        mean = jnp.mean(wide, axis=1, keepdims=True)
        shifted = wide - mean
        inverse = lax.rsqrt(jnp.mean(shifted * shifted, axis=1, keepdims=True) + epsilon)
        mean_ref[rows, :] = mean
        inv_ref[rows, :] = inverse
        normed = (shifted * inverse * gain_ref[...]).astype(jnp.bfloat16)
        normed_ref[rows, :] = normed
        pre_ref[rows, :] = jnp.dot(normed, w_ref[...], preferred_element_type=jnp.float32)
        swap_rows(j).wait_recv()
        chosen[j] = jnp.where(
            flags_ref[rows, :] == 1,
            land_z[j].astype(jnp.float32),
            moved_ref[rows, :].astype(jnp.float32),
        ).astype(jnp.bfloat16)
        share_y(j).start()
        fully_ref[rows, here] = chosen[j]
        return carry

    def finish(j, carry):
        share_y(j).wait_recv()
        fully_ref[rows_of(j), there] = land_y[j]
        swap_rows(j).wait_send()
        share_x(j).wait_send()
        share_y(j).wait_send()
        return carry

    lax.fori_loop(0, 4, begin, 0)
    lax.fori_loop(0, 4, block, 0)
    lax.fori_loop(0, 4, finish, 0)


def gathered_rows(inputs, grad_moved, moved, gain, proj_in):
    rows, half = inputs.shape
    low, full = jnp.bfloat16, jnp.float32
    flags = jnp.repeat(moved[0], BLOCK)[:, None]
    landing = pltpu.VMEM((4, BLOCK, half), low)
    return pl.pallas_call(
        gather_kernel,
        out_shape=(
            jax.ShapeDtypeStruct((rows, 2 * half), low),
            jax.ShapeDtypeStruct((rows, 2 * half), low),
            jax.ShapeDtypeStruct((rows, 2 * half), low),
            jax.ShapeDtypeStruct((rows, proj_in.shape[1]), full),
            jax.ShapeDtypeStruct((rows, 1), full),
            jax.ShapeDtypeStruct((rows, 1), full),
        ),
        in_specs=[pl.BlockSpec(memory_space=pltpu.VMEM)] * 5,
        out_specs=[pl.BlockSpec(memory_space=pltpu.VMEM)] * 6,
        scratch_shapes=[landing] * 4 + [pltpu.SemaphoreType.DMA((4,))] * 6,
        compiler_params=pltpu.CompilerParams(
            collective_id=1, has_side_effects=True, vmem_limit_bytes=48 * 1024 * 1024
        ),
    )(inputs, grad_moved, flags, gain[None, :], proj_in)


def on_device(inputs, grad_moved, moved, segments, input_norm_gain, proj_in, proj_out):
    rows = inputs.shape[0]
    span = 2 * DV + 2 * DQK
    heads_here = proj_in.shape[1] // span
    if lax.axis_size("mp") == 2 and lax.axis_size("dp") == 16:
        full_x, full_dy, normalized_rows, pre, row_mean, inverse_deviation = gathered_rows(
            inputs, grad_moved, moved, input_norm_gain, proj_in
        )
        standardized_input = (full_x.astype(jnp.float32) - row_mean) * inverse_deviation
    else:
        top_bit = lax.axis_size("dp").bit_length() - 2
        blocks = rows // BLOCK
        mine = [grad_moved[j * BLOCK : (j + 1) * BLOCK] for j in range(blocks)]
        theirs = [swapped(block, "dp", top_bit) for block in mine]
        full_x = gathered(inputs)
        full_dy = jnp.concatenate(
            [gathered(jnp.where(moved[0, j] == 1, theirs[j], mine[j])) for j in range(blocks)], axis=0
        )
        xfull = full_x.astype(jnp.float32)
        mean_shifted = xfull - jnp.mean(xfull, axis=1, keepdims=True)
        inverse_deviation = lax.rsqrt(
            jnp.mean(mean_shifted * mean_shifted, axis=1, keepdims=True) + epsilon
        )
        standardized_input = mean_shifted * inverse_deviation
        normalized_rows = (standardized_input * input_norm_gain[None, :]).astype(jnp.bfloat16)
        pre = jnp.dot(normalized_rows, proj_in, preferred_element_type=jnp.float32)
    sig_p = jax.nn.sigmoid(pre)
    acts = (pre * sig_p).astype(jnp.bfloat16)
    grad_mix = lax.dot_general(
        full_dy, proj_out, (((1,), (1,)), ((), ())), preferred_element_type=jnp.float32
    )
    order = jnp.arange(rows, dtype=jnp.int32)
    visible = (
        (segments[:, None] == segments[None, :]) & (order[None, :] <= order[:, None])
    ).astype(jnp.float32)
    mixed, saved = forward_heads(acts, visible, heads_here)
    grad_act = backward_heads(saved, grad_mix, visible, heads_here)
    grad_pre = (grad_act * sig_p * (1.0 + pre * (1.0 - sig_p))).astype(jnp.bfloat16)
    local = inputs.shape[1]
    offset = lax.axis_index("mp") * local
    normed_term = lax.dot_general(
        grad_pre, proj_in, (((1,), (1,)), ((), ())), preferred_element_type=jnp.float32
    ).astype(jnp.bfloat16)
    term_scaled = normed_term.astype(jnp.float32) * input_norm_gain[None, :]
    sums = jnp.stack([jnp.sum(term_scaled, axis=1), jnp.sum(term_scaled * standardized_input, axis=1)])
    if lax.axis_size("mp") == 2 and lax.axis_size("dp") == 16:
        sent = lax.dynamic_slice_in_dim(normed_term, local - offset, local, 1)
        kept = lax.dynamic_slice_in_dim(normed_term, offset, local, 1)
        grad_proj_in, grad_proj_out, other_term, other_sums = reduced(
            normalized_rows, grad_pre, full_dy, mixed, sent, sums
        )
        grad_proj_out = grad_proj_out.T
        sums = sums + other_sums
        grad_normed = kept.astype(jnp.float32) + other_term.astype(jnp.float32)
    else:
        partial_out = lax.dot_general(
            mixed, full_dy, (((0,), (0,)), ((), ())), preferred_element_type=jnp.float32
        )
        grad_proj_out = lax.psum_scatter(
            partial_out.astype(jnp.bfloat16), "dp", scatter_dimension=1, tiled=True
        ).astype(jnp.float32)
        partial_in = lax.dot_general(
            normalized_rows, grad_pre, (((0,), (0,)), ((), ())), preferred_element_type=jnp.float32
        )
        grad_proj_in = lax.psum_scatter(
            partial_in.astype(jnp.bfloat16), "dp", scatter_dimension=0, tiled=True
        ).astype(jnp.float32)
        sums = lax.psum(sums, "mp")
        grad_normed = lax.psum_scatter(
            normed_term, "mp", scatter_dimension=1, tiled=True
        ).astype(jnp.float32)
    means = sums / standardized_input.shape[1]
    here = lambda array: lax.dynamic_slice_in_dim(array, offset, local, 1)
    grad_here = here(full_dy).astype(jnp.float32) + inverse_deviation * (
        grad_normed * here(input_norm_gain[None, :])
        - means[0][:, None]
        - here(standardized_input) * means[1][:, None]
    )
    input_gradient = grad_here.astype(jnp.bfloat16)
    return (input_gradient, grad_proj_in, grad_proj_out)


def solution(mesh):
    return jax.shard_map(
        on_device,
        mesh=mesh,
        in_specs=(
            P("dp", "mp"),
            P("dp", "mp"),
            P("dp", None),
            P("dp"),
            P(),
            P(None, "mp"),
            P("mp", None),
        ),
        out_specs=(P("dp", "mp"), P("dp", "mp"), P("mp", "dp")),
        check_vma=False,
    )
```

```python
import jax
import jax.numpy as jnp
from jax import lax
from jax.experimental import pallas as pl
from jax.experimental.pallas import tpu as pltpu
from jax.sharding import PartitionSpec as P

DV = 128
DQK = 64
BLOCK = 128


epsilon = 1e-05
head_floor = 1.0


def swapped(block, axis, apart):
    count = lax.axis_size(axis)
    route = []
    for low in range(count):
        high = low | 1 << apart
        if high != low and high < count:
            route += [(low, high), (high, low)]
    return lax.ppermute(block, axis, route)


def gathered(block):
    return lax.all_gather(block, "mp", axis=1, tiled=True)


def forward_heads(acts, visible, heads_here):
    span = 2 * DV + 2 * DQK
    rows = acts.shape[0]
    parts = acts.reshape(rows, heads_here, span)
    u_vals = parts[:, :, :DV]
    v_vals = parts[:, :, DV : 2 * DV]
    q_vals = parts[:, :, 2 * DV : 2 * DV + DQK]
    k_vals = parts[:, :, 2 * DV + DQK :]
    scores = jnp.einsum("qhd,khd->hqk", q_vals, k_vals, preferred_element_type=jnp.float32)
    sig_s = jax.nn.sigmoid(scores)
    attend = (scores * sig_s * visible[None]).astype(jnp.bfloat16)
    slope = sig_s * (1.0 + scores * (1.0 - sig_s))
    outvals = jnp.einsum("hqk,khd->qhd", attend, v_vals, preferred_element_type=jnp.float32)
    mean_shifted = outvals - jnp.mean(outvals, axis=-1, keepdims=True)
    head_inv = lax.rsqrt(jnp.mean(mean_shifted * mean_shifted, axis=-1, keepdims=True) + head_floor)
    onorm = mean_shifted * head_inv
    mixed = (onorm * u_vals).astype(jnp.bfloat16).reshape(rows, heads_here * DV)
    saved = (u_vals, v_vals, q_vals, k_vals, attend, slope, onorm, head_inv)
    return (mixed, saved)


def backward_heads(saved, grad_mix, visible, heads_here):
    u_vals, v_vals, q_vals, k_vals, attend, slope, onorm, head_inv = saved
    rows = grad_mix.shape[0]
    grad_mixr = grad_mix.reshape(rows, heads_here, DV)
    grad_u = grad_mixr * onorm
    gon = grad_mixr * u_vals
    grad_o = (
        head_inv
        * (
            gon
            - jnp.mean(gon, axis=-1, keepdims=True)
            - onorm * jnp.mean(gon * onorm, axis=-1, keepdims=True)
        )
    ).astype(jnp.bfloat16)
    grad_att = jnp.einsum("qhd,khd->hqk", grad_o, v_vals, preferred_element_type=jnp.float32)
    grad_v = jnp.einsum("hqk,qhd->khd", attend, grad_o, preferred_element_type=jnp.float32)
    grad_scores = (grad_att * visible[None] * slope).astype(jnp.bfloat16)
    grad_q = jnp.einsum("hqk,khd->qhd", grad_scores, k_vals, preferred_element_type=jnp.float32)
    grad_k = jnp.einsum("hqk,qhd->khd", grad_scores, q_vals, preferred_element_type=jnp.float32)
    grad_act = jnp.concatenate([grad_u, grad_v, grad_q, grad_k], axis=-1)
    return grad_act.reshape(rows, heads_here * (2 * DV + 2 * DQK))


MESH = pl.DeviceIdType.MESH


def reduce_kernel(
    normed_ref, pre_ref, dy_ref, mixed_ref, w_ref, x_ref, mean_ref, inv_ref, gain_ref,
    gin_ref, gout_ref, grad_ref,
    own, send_c, recv_c, send_y, recv_y, keep_y, send_z, from_low, from_high, land_t, land_s,
    send_t, send_s, own_t,
    sem_cs, sem_cr, sem_ys, sem_yr, sem_zs, sem_low, sem_high, sem_xs, sem_xr,
):
    wide = pre_ref.shape[1]
    d = lax.axis_index("dp")
    x = lax.axis_index("mp")
    z = d // 4
    y = (d // 2) % 2
    c = d % 2
    upper = z // 2
    inner = (z + upper) % 2
    core_peer = d + 1 - 2 * c
    y_peer = d + 2 - 4 * y

    barrier = pltpu.get_barrier_semaphore()

    def greet(where):
        pl.semaphore_signal(barrier, inc=1, device_id=where, device_id_type=MESH)

    greet({"dp": core_peer})
    greet({"dp": y_peer})
    greet({"mp": 1 - x})

    @pl.when(z > 0)
    def _():
        greet({"dp": d - 4})

    @pl.when(z < 3)
    def _():
        greet({"dp": d + 4})

    pl.semaphore_wait(barrier, 3 + (z + 3) // 4 + (6 - z) // 4)

    def remote(src, dst, send_sem, recv_sem, where):
        return pltpu.make_async_remote_copy(
            src_ref=src, dst_ref=dst, send_sem=send_sem, recv_sem=recv_sem,
            device_id=where, device_id_type=MESH,
        )

    half = land_t.shape[1]

    def part(side):
        return pl.ds(pl.multiple_of(side * half, half), half)

    def rows_of(j):
        return pl.ds(pl.multiple_of(j * 128, 128), 128)

    def cross_t(j):
        rows = rows_of(j)
        return remote(
            send_t.at[rows], land_t.at[rows], sem_xs.at[j], sem_xr.at[j], {"mp": 1 - x}
        )

    cross_s = remote(send_s, land_s, sem_xs.at[4], sem_xr.at[4], {"mp": 1 - x})

    def standard(rows, side):
        wide_x = x_ref[rows, part(side)].astype(jnp.float32)
        return (wide_x - mean_ref[rows, :]) * inv_ref[rows, :]

    def terms(j, carry):
        rows = rows_of(j)

        def half_term(side):
            term = lax.dot_general(
                pre_ref[rows, :], w_ref[part(side), :], (((1,), (1,)), ((), ())),
                preferred_element_type=jnp.float32,
            ).astype(jnp.bfloat16)
            scaled = term.astype(jnp.float32) * gain_ref[:, part(side)]
            first = jnp.sum(scaled, axis=1, keepdims=True)
            second = jnp.sum(scaled * standard(rows, side), axis=1, keepdims=True)
            return term, first, second

        away, first_a, second_a = half_term(1 - x)
        send_t[rows, :] = away
        cross_t(j).start()
        kept, first_k, second_k = half_term(x)
        own_t[rows, :] = kept
        lane = lax.broadcasted_iota(jnp.int32, (128, 128), 1)
        send_s[rows, :] = jnp.where(lane == 0, first_a + first_k, second_a + second_k)
        return carry

    def gradient(j, carry):
        rows = rows_of(j)
        cross_t(j).wait_recv()
        means = (send_s[rows, :] + land_s[rows, :]) * (1.0 / (2 * half))
        normed_grad = own_t[rows, :].astype(jnp.float32) + land_t[rows, :].astype(jnp.float32)
        grad_ref[rows, :] = (
            dy_ref[rows, part(x)].astype(jnp.float32)
            + inv_ref[rows, :]
            * (
                normed_grad * gain_ref[:, part(x)]
                - means[:, 0:1]
                - standard(rows, x) * means[:, 1:2]
            )
        ).astype(jnp.bfloat16)
        cross_t(j).wait_send()
        return carry

    def target(k):
        v = (3 - k) + (k // 2) * inner * (2 * k - 5)
        return (1 - upper) * v + upper * (3 - v)

    def product(slot, core):
        k = slot % 4
        side = (1 - slot // 4) * (1 - y) + (slot // 4) * y
        chunk = target(k) * 4 + side * 2 + core
        cols = pl.ds(pl.multiple_of(chunk * 128, 128), 128)
        left = lax.dot_general(
            normed_ref[:, cols], pre_ref[...], (((0,), (0,)), ((), ())),
            preferred_element_type=jnp.float32,
        )
        right = lax.dot_general(
            dy_ref[:, cols], mixed_ref[...], (((0,), (0,)), ((), ())),
            preferred_element_type=jnp.float32,
        )
        return left, right

    def to_core(slot):
        return remote(
            send_c.at[slot], recv_c.at[slot], sem_cs.at[slot], sem_cr.at[slot], {"dp": core_peer}
        )

    def to_y(k):
        return remote(send_y.at[k], recv_y.at[k], sem_ys.at[k], sem_yr.at[k], {"dp": y_peer})

    def issue(slot):
        left, right = product(slot, 1 - c)
        send_c[slot, :, :wide] = left.astype(jnp.bfloat16)
        send_c[slot, :, wide:] = right.astype(jnp.bfloat16)
        to_core(slot).start()

    issue(0)

    def step(slot, carry):
        @pl.when(slot < 7)
        def _():
            issue(slot + 1)

        left, right = product(slot, c)
        own[:, :wide] = left
        own[:, wide:] = right
        to_core(slot).wait_recv()

        @pl.when(slot < 4)
        def _():
            send_y[slot] = (own[...] + recv_c[slot].astype(jnp.float32)).astype(jnp.bfloat16)
            to_y(slot).start()

        @pl.when(slot >= 4)
        def _():
            keep_y[slot - 4] = (own[...] + recv_c[slot].astype(jnp.float32)).astype(jnp.bfloat16)

        return carry

    lax.fori_loop(0, 8, step, 0)
    lax.fori_loop(0, 4, terms, 0)
    cross_s.start()

    def up(k, t):
        return remote(send_z.at[k], from_low.at[t], sem_zs.at[k], sem_low.at[t], {"dp": d + 4})

    def down(k, t):
        return remote(send_z.at[k], from_high.at[t], sem_zs.at[k], sem_high.at[t], {"dp": d - 4})

    def along(k, carry):
        t = target(k)
        to_y(k).wait_recv()

        @pl.when(t == z)
        def _():
            own[...] = keep_y[k].astype(jnp.float32) + recv_y[k].astype(jnp.float32)

        def forward(arrived, sem, present, copy):
            @pl.when(present)
            def _():
                pltpu.make_async_copy(arrived.at[t], arrived.at[t], sem.at[t]).wait()
                send_z[k] = (
                    keep_y[k].astype(jnp.float32)
                    + recv_y[k].astype(jnp.float32)
                    + arrived[t].astype(jnp.float32)
                ).astype(jnp.bfloat16)

            @pl.when(jnp.logical_not(present))
            def _():
                send_z[k] = (
                    keep_y[k].astype(jnp.float32) + recv_y[k].astype(jnp.float32)
                ).astype(jnp.bfloat16)

            copy.start()

        @pl.when(t > z)
        def _():
            forward(from_low, sem_low, z > 0, up(k, t))

        @pl.when(t < z)
        def _():
            forward(from_high, sem_high, z < 3, down(k, t))

        return carry

    lax.fori_loop(0, 4, along, 0)
    cross_s.wait()
    lax.fori_loop(0, 4, gradient, 0)

    @pl.when(z > 0)
    def _():
        pltpu.make_async_copy(from_low.at[z], from_low.at[z], sem_low.at[z]).wait()
        own[...] += from_low[z].astype(jnp.float32)

    @pl.when(z < 3)
    def _():
        pltpu.make_async_copy(from_high.at[z], from_high.at[z], sem_high.at[z]).wait()
        own[...] += from_high[z].astype(jnp.float32)

    gin_ref[...] = own[:, :wide]
    gout_ref[...] = own[:, wide:]

    def drain(slot, carry):
        to_core(slot).wait_send()
        return carry

    lax.fori_loop(0, 8, drain, 0)

    def drain_far(k, carry):
        to_y(k).wait_send()
        t = target(k)

        @pl.when(t > z)
        def _():
            up(k, t).wait_send()

        @pl.when(t < z)
        def _():
            down(k, t).wait_send()

        return carry

    lax.fori_loop(0, 4, drain_far, 0)


def reduced(normed, grad_pre, full_dy, mixed, proj_in, full_x, mean, inverse, gain):
    rows, half = full_x.shape[0], full_x.shape[1] // 2
    wide, narrow = grad_pre.shape[1], mixed.shape[1]
    total = wide + narrow
    low, full = jnp.bfloat16, jnp.float32
    return pl.pallas_call(
        reduce_kernel,
        out_shape=(
            jax.ShapeDtypeStruct((128, wide), full),
            jax.ShapeDtypeStruct((128, narrow), full),
            jax.ShapeDtypeStruct((rows, half), low),
        ),
        in_specs=[pl.BlockSpec(memory_space=pltpu.VMEM)] * 9,
        out_specs=[pl.BlockSpec(memory_space=pltpu.VMEM)] * 3,
        scratch_shapes=[
            pltpu.VMEM((128, total), full),
            pltpu.VMEM((8, 128, total), low),
            pltpu.VMEM((8, 128, total), low),
            pltpu.VMEM((4, 128, total), low),
            pltpu.VMEM((4, 128, total), low),
            pltpu.VMEM((4, 128, total), low),
            pltpu.VMEM((4, 128, total), low),
            pltpu.VMEM((4, 128, total), low),
            pltpu.VMEM((4, 128, total), low),
            pltpu.VMEM((rows, half), low),
            pltpu.VMEM((rows, 128), full),
            pltpu.VMEM((rows, half), low),
            pltpu.VMEM((rows, 128), full),
            pltpu.VMEM((rows, half), low),
            pltpu.SemaphoreType.DMA((8,)),
            pltpu.SemaphoreType.DMA((8,)),
            pltpu.SemaphoreType.DMA((4,)),
            pltpu.SemaphoreType.DMA((4,)),
            pltpu.SemaphoreType.DMA((4,)),
            pltpu.SemaphoreType.DMA((4,)),
            pltpu.SemaphoreType.DMA((4,)),
            pltpu.SemaphoreType.DMA((5,)),
            pltpu.SemaphoreType.DMA((5,)),
        ],
        compiler_params=pltpu.CompilerParams(
            collective_id=0, has_side_effects=True, vmem_limit_bytes=60 * 1024 * 1024
        ),
    )(normed, grad_pre, full_dy, mixed, proj_in, full_x, mean, inverse, gain[None, :])


def gather_kernel(
    x_ref, moved_ref, flags_ref, gain_ref, w_ref,
    fullx_ref, fully_ref, normed_ref, pre_ref, mean_ref, inv_ref,
    land_z, land_x, land_y, chosen,
    sem_zs, sem_zr, sem_xs, sem_xr, sem_ys, sem_yr,
):
    d = lax.axis_index("dp")
    m = lax.axis_index("mp")
    half = x_ref.shape[1]
    partner = (d + 8) % 16
    barrier = pltpu.get_barrier_semaphore()
    pl.semaphore_signal(barrier, inc=1, device_id={"dp": partner}, device_id_type=MESH)
    pl.semaphore_signal(barrier, inc=1, device_id={"mp": 1 - m}, device_id_type=MESH)
    pl.semaphore_wait(barrier, 2)
    here = pl.ds(pl.multiple_of(m * half, half), half)
    there = pl.ds(pl.multiple_of((1 - m) * half, half), half)

    def rows_of(j):
        return pl.ds(pl.multiple_of(j * BLOCK, BLOCK), BLOCK)

    def swap_rows(j):
        return pltpu.make_async_remote_copy(
            src_ref=moved_ref.at[rows_of(j)], dst_ref=land_z.at[j],
            send_sem=sem_zs.at[j], recv_sem=sem_zr.at[j],
            device_id={"dp": partner}, device_id_type=MESH,
        )

    def share_x(j):
        return pltpu.make_async_remote_copy(
            src_ref=x_ref.at[rows_of(j)], dst_ref=land_x.at[j],
            send_sem=sem_xs.at[j], recv_sem=sem_xr.at[j],
            device_id={"mp": 1 - m}, device_id_type=MESH,
        )

    def share_y(j):
        return pltpu.make_async_remote_copy(
            src_ref=chosen.at[j], dst_ref=land_y.at[j],
            send_sem=sem_ys.at[j], recv_sem=sem_yr.at[j],
            device_id={"mp": 1 - m}, device_id_type=MESH,
        )

    def begin(j, carry):
        swap_rows(j).start()
        share_x(j).start()
        return carry

    def block(j, carry):
        rows = rows_of(j)
        share_x(j).wait_recv()
        fullx_ref[rows, here] = x_ref[rows, :]
        fullx_ref[rows, there] = land_x[j]
        wide = fullx_ref[rows, :].astype(jnp.float32)
        mean = jnp.mean(wide, axis=1, keepdims=True)
        shifted = wide - mean
        inverse = lax.rsqrt(jnp.mean(shifted * shifted, axis=1, keepdims=True) + epsilon)
        mean_ref[rows, :] = mean
        inv_ref[rows, :] = inverse
        normed = (shifted * inverse * gain_ref[...]).astype(jnp.bfloat16)
        normed_ref[rows, :] = normed
        pre_ref[rows, :] = jnp.dot(normed, w_ref[...], preferred_element_type=jnp.float32)
        swap_rows(j).wait_recv()
        chosen[j] = jnp.where(
            flags_ref[rows, :] == 1,
            land_z[j].astype(jnp.float32),
            moved_ref[rows, :].astype(jnp.float32),
        ).astype(jnp.bfloat16)
        share_y(j).start()
        fully_ref[rows, here] = chosen[j]
        return carry

    def finish(j, carry):
        share_y(j).wait_recv()
        fully_ref[rows_of(j), there] = land_y[j]
        swap_rows(j).wait_send()
        share_x(j).wait_send()
        share_y(j).wait_send()
        return carry

    lax.fori_loop(0, 4, begin, 0)
    lax.fori_loop(0, 4, block, 0)
    lax.fori_loop(0, 4, finish, 0)


def gathered_rows(inputs, grad_moved, moved, gain, proj_in):
    rows, half = inputs.shape
    low, full = jnp.bfloat16, jnp.float32
    flags = jnp.repeat(moved[0], BLOCK)[:, None]
    landing = pltpu.VMEM((4, BLOCK, half), low)
    return pl.pallas_call(
        gather_kernel,
        out_shape=(
            jax.ShapeDtypeStruct((rows, 2 * half), low),
            jax.ShapeDtypeStruct((rows, 2 * half), low),
            jax.ShapeDtypeStruct((rows, 2 * half), low),
            jax.ShapeDtypeStruct((rows, proj_in.shape[1]), full),
            jax.ShapeDtypeStruct((rows, 1), full),
            jax.ShapeDtypeStruct((rows, 1), full),
        ),
        in_specs=[pl.BlockSpec(memory_space=pltpu.VMEM)] * 5,
        out_specs=[pl.BlockSpec(memory_space=pltpu.VMEM)] * 6,
        scratch_shapes=[landing] * 4 + [pltpu.SemaphoreType.DMA((4,))] * 6,
        compiler_params=pltpu.CompilerParams(
            collective_id=1, has_side_effects=True, vmem_limit_bytes=48 * 1024 * 1024
        ),
    )(inputs, grad_moved, flags, gain[None, :], proj_in)


def heads_kernel(pre_ref, dy_ref, w_ref, seg_col_ref, seg_row_ref, grad_ref, mixed_ref):
    low, full = jnp.bfloat16, jnp.float32
    pre = pre_ref[...]
    sig_p = jax.nn.sigmoid(pre)
    act = (pre * sig_p).astype(low)
    slope_p = sig_p * (1.0 + pre * (1.0 - sig_p))
    u_vals = act[:, :DV].astype(full)
    v_vals = act[:, DV : 2 * DV]
    q_vals = act[:, 2 * DV : 2 * DV + DQK]
    k_vals = act[:, 2 * DV + DQK :]

    def dot(a, b, i, j):
        return lax.dot_general(a, b, (((i,), (j,)), ((), ())), preferred_element_type=full)

    scores = dot(q_vals, k_vals, 1, 1)
    shape = scores.shape
    row = lax.broadcasted_iota(jnp.int32, shape, 0)
    col = lax.broadcasted_iota(jnp.int32, shape, 1)
    visible = jnp.where((seg_col_ref[...] == seg_row_ref[...]) & (col <= row), 1.0, 0.0)
    sig_s = jax.nn.sigmoid(scores)
    attend = (scores * sig_s * visible).astype(low)
    slope = sig_s * (1.0 + scores * (1.0 - sig_s)) * visible
    outvals = dot(attend, v_vals, 1, 0)
    shifted = outvals - jnp.mean(outvals, axis=1, keepdims=True)
    head_inv = lax.rsqrt(jnp.mean(shifted * shifted, axis=1, keepdims=True) + head_floor)
    onorm = shifted * head_inv
    mixed_ref[...] = (onorm * u_vals).astype(low)
    grad_mix = dot(dy_ref[...], w_ref[...], 1, 1)
    gon = grad_mix * u_vals
    grad_o = (
        head_inv
        * (
            gon
            - jnp.mean(gon, axis=1, keepdims=True)
            - onorm * jnp.mean(gon * onorm, axis=1, keepdims=True)
        )
    ).astype(low)
    grad_scores = (dot(grad_o, v_vals, 1, 1) * slope).astype(low)
    grad_ref[:, :DV] = (grad_mix * onorm * slope_p[:, :DV]).astype(low)
    grad_ref[:, DV : 2 * DV] = (dot(attend, grad_o, 0, 0) * slope_p[:, DV : 2 * DV]).astype(low)
    grad_qk = jnp.concatenate(
        [dot(grad_scores, k_vals, 1, 0), dot(grad_scores, q_vals, 0, 0)], axis=1
    )
    grad_ref[:, 2 * DV :] = (grad_qk * slope_p[:, 2 * DV :]).astype(low)


def heads_pass(pre, full_dy, proj_out, segments):
    rows, width = pre.shape
    span = 2 * DV + 2 * DQK
    heads_here = width // span
    return pl.pallas_call(
        heads_kernel,
        grid=(heads_here,),
        out_shape=(
            jax.ShapeDtypeStruct((rows, width), jnp.bfloat16),
            jax.ShapeDtypeStruct((rows, heads_here * DV), jnp.bfloat16),
        ),
        in_specs=[
            pl.BlockSpec((rows, span), lambda h: (0, h)),
            pl.BlockSpec(full_dy.shape, lambda h: (0, 0)),
            pl.BlockSpec((DV, proj_out.shape[1]), lambda h: (h, 0)),
            pl.BlockSpec((rows, 1), lambda h: (0, 0)),
            pl.BlockSpec((1, rows), lambda h: (0, 0)),
        ],
        out_specs=[
            pl.BlockSpec((rows, span), lambda h: (0, h)),
            pl.BlockSpec((rows, DV), lambda h: (0, h)),
        ],
        compiler_params=pltpu.CompilerParams(vmem_limit_bytes=40 * 1024 * 1024),
    )(pre, full_dy, proj_out, segments[:, None], segments[None, :])


def on_device(inputs, grad_moved, moved, segments, input_norm_gain, proj_in, proj_out):
    rows = inputs.shape[0]
    span = 2 * DV + 2 * DQK
    heads_here = proj_in.shape[1] // span
    if lax.axis_size("mp") == 2 and lax.axis_size("dp") == 16:
        full_x, full_dy, normalized_rows, pre, row_mean, inverse_deviation = gathered_rows(
            inputs, grad_moved, moved, input_norm_gain, proj_in
        )
        grad_pre, mixed = heads_pass(pre, full_dy, proj_out, segments)
        grad_proj_in, grad_proj_out, input_gradient = reduced(
            normalized_rows, grad_pre, full_dy, mixed, proj_in,
            full_x, row_mean, inverse_deviation, input_norm_gain,
        )
        return (input_gradient, grad_proj_in, grad_proj_out.T)
    top_bit = lax.axis_size("dp").bit_length() - 2
    blocks = rows // BLOCK
    mine = [grad_moved[j * BLOCK : (j + 1) * BLOCK] for j in range(blocks)]
    theirs = [swapped(block, "dp", top_bit) for block in mine]
    full_x = gathered(inputs)
    full_dy = jnp.concatenate(
        [gathered(jnp.where(moved[0, j] == 1, theirs[j], mine[j])) for j in range(blocks)], axis=0
    )
    xfull = full_x.astype(jnp.float32)
    mean_shifted = xfull - jnp.mean(xfull, axis=1, keepdims=True)
    inverse_deviation = lax.rsqrt(
        jnp.mean(mean_shifted * mean_shifted, axis=1, keepdims=True) + epsilon
    )
    standardized_input = mean_shifted * inverse_deviation
    normalized_rows = (standardized_input * input_norm_gain[None, :]).astype(jnp.bfloat16)
    pre = jnp.dot(normalized_rows, proj_in, preferred_element_type=jnp.float32)
    sig_p = jax.nn.sigmoid(pre)
    acts = (pre * sig_p).astype(jnp.bfloat16)
    grad_mix = lax.dot_general(
        full_dy, proj_out, (((1,), (1,)), ((), ())), preferred_element_type=jnp.float32
    )
    order = jnp.arange(rows, dtype=jnp.int32)
    visible = (
        (segments[:, None] == segments[None, :]) & (order[None, :] <= order[:, None])
    ).astype(jnp.float32)
    mixed, saved = forward_heads(acts, visible, heads_here)
    grad_act = backward_heads(saved, grad_mix, visible, heads_here)
    grad_pre = (grad_act * sig_p * (1.0 + pre * (1.0 - sig_p))).astype(jnp.bfloat16)
    local = inputs.shape[1]
    offset = lax.axis_index("mp") * local
    normed_term = lax.dot_general(
        grad_pre, proj_in, (((1,), (1,)), ((), ())), preferred_element_type=jnp.float32
    ).astype(jnp.bfloat16)
    term_scaled = normed_term.astype(jnp.float32) * input_norm_gain[None, :]
    sums = jnp.stack([jnp.sum(term_scaled, axis=1), jnp.sum(term_scaled * standardized_input, axis=1)])
    partial_out = lax.dot_general(
        mixed, full_dy, (((0,), (0,)), ((), ())), preferred_element_type=jnp.float32
    )
    grad_proj_out = lax.psum_scatter(
        partial_out.astype(jnp.bfloat16), "dp", scatter_dimension=1, tiled=True
    ).astype(jnp.float32)
    partial_in = lax.dot_general(
        normalized_rows, grad_pre, (((0,), (0,)), ((), ())), preferred_element_type=jnp.float32
    )
    grad_proj_in = lax.psum_scatter(
        partial_in.astype(jnp.bfloat16), "dp", scatter_dimension=0, tiled=True
    ).astype(jnp.float32)
    sums = lax.psum(sums, "mp")
    grad_normed = lax.psum_scatter(
        normed_term, "mp", scatter_dimension=1, tiled=True
    ).astype(jnp.float32)
    means = sums / standardized_input.shape[1]
    here = lambda array: lax.dynamic_slice_in_dim(array, offset, local, 1)
    grad_here = here(full_dy).astype(jnp.float32) + inverse_deviation * (
        grad_normed * here(input_norm_gain[None, :])
        - means[0][:, None]
        - here(standardized_input) * means[1][:, None]
    )
    input_gradient = grad_here.astype(jnp.bfloat16)
    return (input_gradient, grad_proj_in, grad_proj_out)


def solution(mesh):
    return jax.shard_map(
        on_device,
        mesh=mesh,
        in_specs=(
            P("dp", "mp"),
            P("dp", "mp"),
            P("dp", None),
            P("dp"),
            P(),
            P(None, "mp"),
            P("mp", None),
        ),
        out_specs=(P("dp", "mp"), P("dp", "mp"), P("mp", "dp")),
        check_vma=False,
    )
```

```python
import jax
import jax.numpy as jnp
from jax import lax
from jax.experimental import pallas as pl
from jax.experimental.pallas import tpu as pltpu
from jax.sharding import PartitionSpec as P

DV = 128
DQK = 64
BLOCK = 128


epsilon = 1e-05
head_floor = 1.0


def swapped(block, axis, apart):
    count = lax.axis_size(axis)
    route = []
    for low in range(count):
        high = low | 1 << apart
        if high != low and high < count:
            route += [(low, high), (high, low)]
    return lax.ppermute(block, axis, route)


def gathered(block):
    return lax.all_gather(block, "mp", axis=1, tiled=True)


def forward_heads(acts, visible, heads_here):
    span = 2 * DV + 2 * DQK
    rows = acts.shape[0]
    parts = acts.reshape(rows, heads_here, span)
    u_vals = parts[:, :, :DV]
    v_vals = parts[:, :, DV : 2 * DV]
    q_vals = parts[:, :, 2 * DV : 2 * DV + DQK]
    k_vals = parts[:, :, 2 * DV + DQK :]
    scores = jnp.einsum("qhd,khd->hqk", q_vals, k_vals, preferred_element_type=jnp.float32)
    sig_s = jax.nn.sigmoid(scores)
    attend = (scores * sig_s * visible[None]).astype(jnp.bfloat16)
    slope = sig_s * (1.0 + scores * (1.0 - sig_s))
    outvals = jnp.einsum("hqk,khd->qhd", attend, v_vals, preferred_element_type=jnp.float32)
    mean_shifted = outvals - jnp.mean(outvals, axis=-1, keepdims=True)
    head_inv = lax.rsqrt(jnp.mean(mean_shifted * mean_shifted, axis=-1, keepdims=True) + head_floor)
    onorm = mean_shifted * head_inv
    mixed = (onorm * u_vals).astype(jnp.bfloat16).reshape(rows, heads_here * DV)
    saved = (u_vals, v_vals, q_vals, k_vals, attend, slope, onorm, head_inv)
    return (mixed, saved)


def backward_heads(saved, grad_mix, visible, heads_here):
    u_vals, v_vals, q_vals, k_vals, attend, slope, onorm, head_inv = saved
    rows = grad_mix.shape[0]
    grad_mixr = grad_mix.reshape(rows, heads_here, DV)
    grad_u = grad_mixr * onorm
    gon = grad_mixr * u_vals
    grad_o = (
        head_inv
        * (
            gon
            - jnp.mean(gon, axis=-1, keepdims=True)
            - onorm * jnp.mean(gon * onorm, axis=-1, keepdims=True)
        )
    ).astype(jnp.bfloat16)
    grad_att = jnp.einsum("qhd,khd->hqk", grad_o, v_vals, preferred_element_type=jnp.float32)
    grad_v = jnp.einsum("hqk,qhd->khd", attend, grad_o, preferred_element_type=jnp.float32)
    grad_scores = (grad_att * visible[None] * slope).astype(jnp.bfloat16)
    grad_q = jnp.einsum("hqk,khd->qhd", grad_scores, k_vals, preferred_element_type=jnp.float32)
    grad_k = jnp.einsum("hqk,qhd->khd", grad_scores, q_vals, preferred_element_type=jnp.float32)
    grad_act = jnp.concatenate([grad_u, grad_v, grad_q, grad_k], axis=-1)
    return grad_act.reshape(rows, heads_here * (2 * DV + 2 * DQK))


MESH = pl.DeviceIdType.MESH


def reduce_kernel(
    normed_ref, pre_ref, dy_ref, mixed_ref, w_ref, x_ref, mean_ref, inv_ref, gain_ref,
    gin_ref, gout_ref, grad_ref,
    own, send_c, recv_c, send_y, recv_y, keep_y, send_z, from_low, from_high, land_t, land_s,
    send_t, send_s, own_t,
    sem_cs, sem_cr, sem_ys, sem_yr, sem_zs, sem_low, sem_high, sem_xs, sem_xr,
):
    wide = pre_ref.shape[1]
    d = lax.axis_index("dp")
    x = lax.axis_index("mp")
    z = d // 4
    y = (d // 2) % 2
    c = d % 2
    upper = z // 2
    inner = (z + upper) % 2
    core_peer = d + 1 - 2 * c
    y_peer = d + 2 - 4 * y

    barrier = pltpu.get_barrier_semaphore()

    def greet(where):
        pl.semaphore_signal(barrier, inc=1, device_id=where, device_id_type=MESH)

    greet({"dp": core_peer})
    greet({"dp": y_peer})
    greet({"mp": 1 - x})

    @pl.when(z > 0)
    def _():
        greet({"dp": d - 4})

    @pl.when(z < 3)
    def _():
        greet({"dp": d + 4})

    pl.semaphore_wait(barrier, 3 + (z + 3) // 4 + (6 - z) // 4)

    def remote(src, dst, send_sem, recv_sem, where):
        return pltpu.make_async_remote_copy(
            src_ref=src, dst_ref=dst, send_sem=send_sem, recv_sem=recv_sem,
            device_id=where, device_id_type=MESH,
        )

    half = land_t.shape[1]

    def part(side):
        return pl.ds(pl.multiple_of(side * half, half), half)

    def rows_of(j):
        return pl.ds(pl.multiple_of(j * 128, 128), 128)

    def cross_t(j):
        rows = rows_of(j)
        return remote(
            send_t.at[rows], land_t.at[rows], sem_xs.at[j], sem_xr.at[j], {"mp": 1 - x}
        )

    cross_s = remote(send_s, land_s, sem_xs.at[4], sem_xr.at[4], {"mp": 1 - x})

    def standard(rows, side):
        wide_x = x_ref[rows, part(side)].astype(jnp.float32)
        return (wide_x - mean_ref[rows, :]) * inv_ref[rows, :]

    def terms(j, carry):
        rows = rows_of(j)

        def half_term(side):
            term = lax.dot_general(
                pre_ref[rows, :], w_ref[part(side), :], (((1,), (1,)), ((), ())),
                preferred_element_type=jnp.float32,
            ).astype(jnp.bfloat16)
            scaled = term.astype(jnp.float32) * gain_ref[:, part(side)]
            first = jnp.sum(scaled, axis=1, keepdims=True)
            second = jnp.sum(scaled * standard(rows, side), axis=1, keepdims=True)
            return term, first, second

        away, first_a, second_a = half_term(1 - x)
        send_t[rows, :] = away
        cross_t(j).start()
        kept, first_k, second_k = half_term(x)
        own_t[rows, :] = kept
        lane = lax.broadcasted_iota(jnp.int32, (128, 128), 1)
        send_s[rows, :] = jnp.where(lane == 0, first_a + first_k, second_a + second_k)
        return carry

    def gradient(j, carry):
        rows = rows_of(j)
        cross_t(j).wait_recv()
        means = (send_s[rows, :] + land_s[rows, :]) * (1.0 / (2 * half))
        normed_grad = own_t[rows, :].astype(jnp.float32) + land_t[rows, :].astype(jnp.float32)
        grad_ref[rows, :] = (
            dy_ref[rows, part(x)].astype(jnp.float32)
            + inv_ref[rows, :]
            * (
                normed_grad * gain_ref[:, part(x)]
                - means[:, 0:1]
                - standard(rows, x) * means[:, 1:2]
            )
        ).astype(jnp.bfloat16)
        cross_t(j).wait_send()
        return carry

    def target(k):
        v = (3 - k) + (k // 2) * inner * (2 * k - 5)
        return (1 - upper) * v + upper * (3 - v)

    def product(slot, core):
        k = slot % 4
        side = (1 - slot // 4) * (1 - y) + (slot // 4) * y
        chunk = target(k) * 4 + side * 2 + core
        cols = pl.ds(pl.multiple_of(chunk * 128, 128), 128)
        left = lax.dot_general(
            normed_ref[:, cols], pre_ref[...], (((0,), (0,)), ((), ())),
            preferred_element_type=jnp.float32,
        )
        right = lax.dot_general(
            dy_ref[:, cols], mixed_ref[...], (((0,), (0,)), ((), ())),
            preferred_element_type=jnp.float32,
        )
        return left, right

    def to_core(slot):
        return remote(
            send_c.at[slot], recv_c.at[slot], sem_cs.at[slot], sem_cr.at[slot], {"dp": core_peer}
        )

    def to_y(k):
        return remote(send_y.at[k], recv_y.at[k], sem_ys.at[k], sem_yr.at[k], {"dp": y_peer})

    def issue(slot):
        left, right = product(slot, 1 - c)
        send_c[slot, :, :wide] = left.astype(jnp.bfloat16)
        send_c[slot, :, wide:] = right.astype(jnp.bfloat16)
        to_core(slot).start()

    issue(0)

    def step(slot, carry):
        @pl.when(slot < 7)
        def _():
            issue(slot + 1)

        left, right = product(slot, c)
        own[:, :wide] = left
        own[:, wide:] = right
        to_core(slot).wait_recv()

        @pl.when(slot < 4)
        def _():
            send_y[slot] = (own[...] + recv_c[slot].astype(jnp.float32)).astype(jnp.bfloat16)
            to_y(slot).start()

        @pl.when(slot >= 4)
        def _():
            keep_y[slot - 4] = (own[...] + recv_c[slot].astype(jnp.float32)).astype(jnp.bfloat16)

        return carry

    lax.fori_loop(0, 8, step, 0)
    lax.fori_loop(0, 4, terms, 0)
    cross_s.start()

    def up(k, t):
        return remote(send_z.at[k], from_low.at[t], sem_zs.at[k], sem_low.at[t], {"dp": d + 4})

    def down(k, t):
        return remote(send_z.at[k], from_high.at[t], sem_zs.at[k], sem_high.at[t], {"dp": d - 4})

    def along(k, carry):
        t = target(k)
        to_y(k).wait_recv()

        @pl.when(t == z)
        def _():
            own[...] = keep_y[k].astype(jnp.float32) + recv_y[k].astype(jnp.float32)

        def forward(arrived, sem, present, copy):
            @pl.when(present)
            def _():
                pltpu.make_async_copy(arrived.at[t], arrived.at[t], sem.at[t]).wait()
                send_z[k] = (
                    keep_y[k].astype(jnp.float32)
                    + recv_y[k].astype(jnp.float32)
                    + arrived[t].astype(jnp.float32)
                ).astype(jnp.bfloat16)

            @pl.when(jnp.logical_not(present))
            def _():
                send_z[k] = (
                    keep_y[k].astype(jnp.float32) + recv_y[k].astype(jnp.float32)
                ).astype(jnp.bfloat16)

            copy.start()

        @pl.when(t > z)
        def _():
            forward(from_low, sem_low, z > 0, up(k, t))

        @pl.when(t < z)
        def _():
            forward(from_high, sem_high, z < 3, down(k, t))

        return carry

    lax.fori_loop(0, 4, along, 0)
    cross_s.wait()
    lax.fori_loop(0, 4, gradient, 0)

    @pl.when(z > 0)
    def _():
        pltpu.make_async_copy(from_low.at[z], from_low.at[z], sem_low.at[z]).wait()
        own[...] += from_low[z].astype(jnp.float32)

    @pl.when(z < 3)
    def _():
        pltpu.make_async_copy(from_high.at[z], from_high.at[z], sem_high.at[z]).wait()
        own[...] += from_high[z].astype(jnp.float32)

    gin_ref[...] = own[:, :wide]
    gout_ref[...] = own[:, wide:]

    def drain(slot, carry):
        to_core(slot).wait_send()
        return carry

    lax.fori_loop(0, 8, drain, 0)

    def drain_far(k, carry):
        to_y(k).wait_send()
        t = target(k)

        @pl.when(t > z)
        def _():
            up(k, t).wait_send()

        @pl.when(t < z)
        def _():
            down(k, t).wait_send()

        return carry

    lax.fori_loop(0, 4, drain_far, 0)


def reduced(normed, grad_pre, full_dy, mixed, proj_in, full_x, mean, inverse, gain):
    rows, half = full_x.shape[0], full_x.shape[1] // 2
    wide, narrow = grad_pre.shape[1], mixed.shape[1]
    total = wide + narrow
    low, full = jnp.bfloat16, jnp.float32
    return pl.pallas_call(
        reduce_kernel,
        out_shape=(
            jax.ShapeDtypeStruct((128, wide), full),
            jax.ShapeDtypeStruct((128, narrow), full),
            jax.ShapeDtypeStruct((rows, half), low),
        ),
        in_specs=[pl.BlockSpec(memory_space=pltpu.VMEM)] * 9,
        out_specs=[pl.BlockSpec(memory_space=pltpu.VMEM)] * 3,
        scratch_shapes=[
            pltpu.VMEM((128, total), full),
            pltpu.VMEM((8, 128, total), low),
            pltpu.VMEM((8, 128, total), low),
            pltpu.VMEM((4, 128, total), low),
            pltpu.VMEM((4, 128, total), low),
            pltpu.VMEM((4, 128, total), low),
            pltpu.VMEM((4, 128, total), low),
            pltpu.VMEM((4, 128, total), low),
            pltpu.VMEM((4, 128, total), low),
            pltpu.VMEM((rows, half), low),
            pltpu.VMEM((rows, 128), full),
            pltpu.VMEM((rows, half), low),
            pltpu.VMEM((rows, 128), full),
            pltpu.VMEM((rows, half), low),
            pltpu.SemaphoreType.DMA((8,)),
            pltpu.SemaphoreType.DMA((8,)),
            pltpu.SemaphoreType.DMA((4,)),
            pltpu.SemaphoreType.DMA((4,)),
            pltpu.SemaphoreType.DMA((4,)),
            pltpu.SemaphoreType.DMA((4,)),
            pltpu.SemaphoreType.DMA((4,)),
            pltpu.SemaphoreType.DMA((5,)),
            pltpu.SemaphoreType.DMA((5,)),
        ],
        compiler_params=pltpu.CompilerParams(
            collective_id=0, has_side_effects=True, vmem_limit_bytes=60 * 1024 * 1024
        ),
    )(normed, grad_pre, full_dy, mixed, proj_in, full_x, mean, inverse, gain[None, :])


def gather_kernel(
    x_ref, moved_ref, flags_ref, gain_ref, w_ref,
    fullx_ref, fully_ref, normed_ref, pre_ref, mean_ref, inv_ref,
    land_z, land_x, land_y, chosen,
    sem_zs, sem_zr, sem_xs, sem_xr, sem_ys, sem_yr,
):
    d = lax.axis_index("dp")
    m = lax.axis_index("mp")
    half = x_ref.shape[1]
    partner = (d + 8) % 16
    barrier = pltpu.get_barrier_semaphore()
    pl.semaphore_signal(barrier, inc=1, device_id={"dp": partner}, device_id_type=MESH)
    pl.semaphore_signal(barrier, inc=1, device_id={"mp": 1 - m}, device_id_type=MESH)
    pl.semaphore_wait(barrier, 2)
    here = pl.ds(pl.multiple_of(m * half, half), half)
    there = pl.ds(pl.multiple_of((1 - m) * half, half), half)

    def rows_of(j):
        return pl.ds(pl.multiple_of(j * BLOCK, BLOCK), BLOCK)

    def swap_rows(j):
        return pltpu.make_async_remote_copy(
            src_ref=moved_ref.at[rows_of(j)], dst_ref=land_z.at[j],
            send_sem=sem_zs.at[j], recv_sem=sem_zr.at[j],
            device_id={"dp": partner}, device_id_type=MESH,
        )

    def share_x(j):
        return pltpu.make_async_remote_copy(
            src_ref=x_ref.at[rows_of(j)], dst_ref=land_x.at[j],
            send_sem=sem_xs.at[j], recv_sem=sem_xr.at[j],
            device_id={"mp": 1 - m}, device_id_type=MESH,
        )

    def share_y(j):
        return pltpu.make_async_remote_copy(
            src_ref=chosen.at[j], dst_ref=land_y.at[j],
            send_sem=sem_ys.at[j], recv_sem=sem_yr.at[j],
            device_id={"mp": 1 - m}, device_id_type=MESH,
        )

    def begin(j, carry):
        swap_rows(j).start()
        share_x(j).start()
        return carry

    def block(j, carry):
        rows = rows_of(j)
        share_x(j).wait_recv()
        fullx_ref[rows, here] = x_ref[rows, :]
        fullx_ref[rows, there] = land_x[j]
        wide = fullx_ref[rows, :].astype(jnp.float32)
        mean = jnp.mean(wide, axis=1, keepdims=True)
        shifted = wide - mean
        inverse = lax.rsqrt(jnp.mean(shifted * shifted, axis=1, keepdims=True) + epsilon)
        mean_ref[rows, :] = mean
        inv_ref[rows, :] = inverse
        normed = (shifted * inverse * gain_ref[...]).astype(jnp.bfloat16)
        normed_ref[rows, :] = normed
        pre_ref[rows, :] = jnp.dot(normed, w_ref[...], preferred_element_type=jnp.float32)
        swap_rows(j).wait_recv()
        chosen[j] = jnp.where(
            flags_ref[rows, :] == 1,
            land_z[j].astype(jnp.float32),
            moved_ref[rows, :].astype(jnp.float32),
        ).astype(jnp.bfloat16)
        share_y(j).start()
        fully_ref[rows, here] = chosen[j]
        return carry

    def finish(j, carry):
        share_y(j).wait_recv()
        fully_ref[rows_of(j), there] = land_y[j]
        swap_rows(j).wait_send()
        share_x(j).wait_send()
        share_y(j).wait_send()
        return carry

    lax.fori_loop(0, 4, begin, 0)
    lax.fori_loop(0, 4, block, 0)
    lax.fori_loop(0, 4, finish, 0)


def gathered_rows(inputs, grad_moved, moved, gain, proj_in):
    rows, half = inputs.shape
    low, full = jnp.bfloat16, jnp.float32
    flags = jnp.repeat(moved[0], BLOCK)[:, None]
    landing = pltpu.VMEM((4, BLOCK, half), low)
    return pl.pallas_call(
        gather_kernel,
        out_shape=(
            jax.ShapeDtypeStruct((rows, 2 * half), low),
            jax.ShapeDtypeStruct((rows, 2 * half), low),
            jax.ShapeDtypeStruct((rows, 2 * half), low),
            jax.ShapeDtypeStruct((rows, proj_in.shape[1]), full),
            jax.ShapeDtypeStruct((rows, 1), full),
            jax.ShapeDtypeStruct((rows, 1), full),
        ),
        in_specs=[pl.BlockSpec(memory_space=pltpu.VMEM)] * 5,
        out_specs=[pl.BlockSpec(memory_space=pltpu.VMEM)] * 6,
        scratch_shapes=[landing] * 4 + [pltpu.SemaphoreType.DMA((4,))] * 6,
        compiler_params=pltpu.CompilerParams(
            collective_id=1, has_side_effects=True, vmem_limit_bytes=30 * 1024 * 1024
        ),
    )(inputs, grad_moved, flags, gain[None, :], proj_in)


def heads_kernel(pre_ref, dy_ref, w_ref, seg_col_ref, seg_row_ref, grad_ref, mixed_ref):
    low, full = jnp.bfloat16, jnp.float32
    pre = pre_ref[...]
    sig_p = jax.nn.sigmoid(pre)
    act = (pre * sig_p).astype(low)
    slope_p = sig_p * (1.0 + pre * (1.0 - sig_p))
    u_vals = act[:, :DV].astype(full)
    v_vals = act[:, DV : 2 * DV]
    q_vals = act[:, 2 * DV : 2 * DV + DQK]
    k_vals = act[:, 2 * DV + DQK :]

    def dot(a, b, i, j):
        return lax.dot_general(a, b, (((i,), (j,)), ((), ())), preferred_element_type=full)

    scores = dot(q_vals, k_vals, 1, 1)
    shape = scores.shape
    row = lax.broadcasted_iota(jnp.int32, shape, 0)
    col = lax.broadcasted_iota(jnp.int32, shape, 1)
    visible = jnp.where((seg_col_ref[...] == seg_row_ref[...]) & (col <= row), 1.0, 0.0)
    sig_s = jax.nn.sigmoid(scores)
    attend = (scores * sig_s * visible).astype(low)
    slope = sig_s * (1.0 + scores * (1.0 - sig_s)) * visible
    outvals = dot(attend, v_vals, 1, 0)
    shifted = outvals - jnp.mean(outvals, axis=1, keepdims=True)
    head_inv = lax.rsqrt(jnp.mean(shifted * shifted, axis=1, keepdims=True) + head_floor)
    onorm = shifted * head_inv
    mixed_ref[...] = (onorm * u_vals).astype(low)
    grad_mix = dot(dy_ref[...], w_ref[...], 1, 1)
    gon = grad_mix * u_vals
    grad_o = (
        head_inv
        * (
            gon
            - jnp.mean(gon, axis=1, keepdims=True)
            - onorm * jnp.mean(gon * onorm, axis=1, keepdims=True)
        )
    ).astype(low)
    grad_scores = (dot(grad_o, v_vals, 1, 1) * slope).astype(low)
    grad_ref[:, :DV] = (grad_mix * onorm * slope_p[:, :DV]).astype(low)
    grad_ref[:, DV : 2 * DV] = (dot(attend, grad_o, 0, 0) * slope_p[:, DV : 2 * DV]).astype(low)
    grad_qk = jnp.concatenate(
        [dot(grad_scores, k_vals, 1, 0), dot(grad_scores, q_vals, 0, 0)], axis=1
    )
    grad_ref[:, 2 * DV :] = (grad_qk * slope_p[:, 2 * DV :]).astype(low)


def heads_pass(pre, full_dy, proj_out, segments):
    rows, width = pre.shape
    span = 2 * DV + 2 * DQK
    heads_here = width // span
    return pl.pallas_call(
        heads_kernel,
        grid=(heads_here,),
        out_shape=(
            jax.ShapeDtypeStruct((rows, width), jnp.bfloat16),
            jax.ShapeDtypeStruct((rows, heads_here * DV), jnp.bfloat16),
        ),
        in_specs=[
            pl.BlockSpec((rows, span), lambda h: (0, h)),
            pl.BlockSpec(full_dy.shape, lambda h: (0, 0)),
            pl.BlockSpec((DV, proj_out.shape[1]), lambda h: (h, 0)),
            pl.BlockSpec((rows, 1), lambda h: (0, 0)),
            pl.BlockSpec((1, rows), lambda h: (0, 0)),
        ],
        out_specs=[
            pl.BlockSpec((rows, span), lambda h: (0, h)),
            pl.BlockSpec((rows, DV), lambda h: (0, h)),
        ],
        compiler_params=pltpu.CompilerParams(vmem_limit_bytes=26 * 1024 * 1024),
    )(pre, full_dy, proj_out, segments[:, None], segments[None, :])


def on_device(inputs, grad_moved, moved, segments, input_norm_gain, proj_in, proj_out):
    rows = inputs.shape[0]
    span = 2 * DV + 2 * DQK
    heads_here = proj_in.shape[1] // span
    if lax.axis_size("mp") == 2 and lax.axis_size("dp") == 16:
        full_x, full_dy, normalized_rows, pre, row_mean, inverse_deviation = gathered_rows(
            inputs, grad_moved, moved, input_norm_gain, proj_in
        )
        grad_pre, mixed = heads_pass(pre, full_dy, proj_out, segments)
        grad_proj_in, grad_proj_out, input_gradient = reduced(
            normalized_rows, grad_pre, full_dy, mixed, proj_in,
            full_x, row_mean, inverse_deviation, input_norm_gain,
        )
        return (input_gradient, grad_proj_in, grad_proj_out.T)
    top_bit = lax.axis_size("dp").bit_length() - 2
    blocks = rows // BLOCK
    mine = [grad_moved[j * BLOCK : (j + 1) * BLOCK] for j in range(blocks)]
    theirs = [swapped(block, "dp", top_bit) for block in mine]
    full_x = gathered(inputs)
    full_dy = jnp.concatenate(
        [gathered(jnp.where(moved[0, j] == 1, theirs[j], mine[j])) for j in range(blocks)], axis=0
    )
    xfull = full_x.astype(jnp.float32)
    mean_shifted = xfull - jnp.mean(xfull, axis=1, keepdims=True)
    inverse_deviation = lax.rsqrt(
        jnp.mean(mean_shifted * mean_shifted, axis=1, keepdims=True) + epsilon
    )
    standardized_input = mean_shifted * inverse_deviation
    normalized_rows = (standardized_input * input_norm_gain[None, :]).astype(jnp.bfloat16)
    pre = jnp.dot(normalized_rows, proj_in, preferred_element_type=jnp.float32)
    sig_p = jax.nn.sigmoid(pre)
    acts = (pre * sig_p).astype(jnp.bfloat16)
    grad_mix = lax.dot_general(
        full_dy, proj_out, (((1,), (1,)), ((), ())), preferred_element_type=jnp.float32
    )
    order = jnp.arange(rows, dtype=jnp.int32)
    visible = (
        (segments[:, None] == segments[None, :]) & (order[None, :] <= order[:, None])
    ).astype(jnp.float32)
    mixed, saved = forward_heads(acts, visible, heads_here)
    grad_act = backward_heads(saved, grad_mix, visible, heads_here)
    grad_pre = (grad_act * sig_p * (1.0 + pre * (1.0 - sig_p))).astype(jnp.bfloat16)
    local = inputs.shape[1]
    offset = lax.axis_index("mp") * local
    normed_term = lax.dot_general(
        grad_pre, proj_in, (((1,), (1,)), ((), ())), preferred_element_type=jnp.float32
    ).astype(jnp.bfloat16)
    term_scaled = normed_term.astype(jnp.float32) * input_norm_gain[None, :]
    sums = jnp.stack([jnp.sum(term_scaled, axis=1), jnp.sum(term_scaled * standardized_input, axis=1)])
    partial_out = lax.dot_general(
        mixed, full_dy, (((0,), (0,)), ((), ())), preferred_element_type=jnp.float32
    )
    grad_proj_out = lax.psum_scatter(
        partial_out.astype(jnp.bfloat16), "dp", scatter_dimension=1, tiled=True
    ).astype(jnp.float32)
    partial_in = lax.dot_general(
        normalized_rows, grad_pre, (((0,), (0,)), ((), ())), preferred_element_type=jnp.float32
    )
    grad_proj_in = lax.psum_scatter(
        partial_in.astype(jnp.bfloat16), "dp", scatter_dimension=0, tiled=True
    ).astype(jnp.float32)
    sums = lax.psum(sums, "mp")
    grad_normed = lax.psum_scatter(
        normed_term, "mp", scatter_dimension=1, tiled=True
    ).astype(jnp.float32)
    means = sums / standardized_input.shape[1]
    here = lambda array: lax.dynamic_slice_in_dim(array, offset, local, 1)
    grad_here = here(full_dy).astype(jnp.float32) + inverse_deviation * (
        grad_normed * here(input_norm_gain[None, :])
        - means[0][:, None]
        - here(standardized_input) * means[1][:, None]
    )
    input_gradient = grad_here.astype(jnp.bfloat16)
    return (input_gradient, grad_proj_in, grad_proj_out)


def solution(mesh):
    return jax.shard_map(
        on_device,
        mesh=mesh,
        in_specs=(
            P("dp", "mp"),
            P("dp", "mp"),
            P("dp", None),
            P("dp"),
            P(),
            P(None, "mp"),
            P("mp", None),
        ),
        out_specs=(P("dp", "mp"), P("dp", "mp"), P("mp", "dp")),
        check_vma=False,
    )
```
